32 devices in a mesh: sec: 4 (over z), tile: 4 (over y, core), role: 2 (over x).
Axes of the slice: x: 2, y: 2, z: 4, core: 2. Of those that a mesh axis runs over, the one named last changes fastest.
Arguments:
- pressure: float32 [32, 256, 8192], P(None, 'sec', ('tile', 'role')), may hold values from -6 to 6
- cell_weight: float32 [8192], P(('tile', 'role')), may hold values from 0.25 to 4
- live_cells: int32 [8], replicated, may hold values from 341 to 1024, as said below
- mode_order: int32 [128], replicated, may hold values from 0 to 127, each once
Outputs:
- gram: float32 [128, 32, 32], P('sec', ('tile', 'role'))
The draws below stay inside these ranges and needn't reach their ends.
Inputs may be any that keep to these rules, and one draw needn't show every extreme that they name: `live_cells`: at least one tile half is full. `mode_order`: each wavenumber appears once.
All inputs are finite; a program needn't handle non-finite values.
Results may differ from the reference program's by a relative error of at most 0.0003.
Values sent between devices are 32-bit elements; how exact they have to be, the bound alone decides.
A program may use at most 128 MiB of HBM per device.

```python
import math
import jax
import jax.numpy as jnp
from jax import lax

NS = 32
THETA = 256
NF = 16
MODES = 128
GCELLS = 1024
GROUPS = 8
CELLS = 8192


def draw_live_cells(key, part):
    counts = jax.random.randint(jax.random.fold_in(key, 11), (GROUPS,), GCELLS // 3, GCELLS + 1)
    chosen = jax.random.randint(jax.random.fold_in(key, 12), (), 0, GROUPS)
    return jnp.where(jnp.arange(GROUPS) == chosen, GCELLS, counts).astype(jnp.int32)


def block_scale(rng, shape, cuts, low, top_value):
    level = 1.0
    for axis_at, shards_of in cuts:
        draws = jax.random.uniform(jax.random.fold_in(jax.random.fold_in(rng, 6), axis_at), (shards_of,), jnp.float32, low / len(cuts), top_value / len(cuts))
        level = level * jnp.repeat(jnp.exp(draws), shape[axis_at] // shards_of).reshape((-1,) + (1,) * (len(shape) - 1 - axis_at))
    return level


def normal_values(rng, extent, scale, most, cuts=(), kind=jnp.bfloat16):
    array = scale * jax.random.normal(rng, extent, jnp.float32)
    if cuts:
        array = array * block_scale(rng, extent, cuts, -0.22, 0.18)
    return jnp.clip(array, -most, most).astype(kind)


def setup_inputs(seed: int = 0) -> dict:
    key_of = jax.random.split(jax.random.key(seed), 5)
    return {
        "pressure": normal_values(key_of[0], (NS, THETA, CELLS), 1.0, 6.0, ((1, 4), (2, 8)), jnp.float32),
        "cell_weight": jnp.clip(jnp.exp(math.log(4.0) - 2.7725887 * jax.random.uniform(key_of[1], (CELLS,), jnp.float32) ** block_scale(key_of[1], (CELLS,), ((0, 8),), -0.2, 0.2)), 0.25, 4.0),
        "live_cells": draw_live_cells(jax.random.fold_in(key_of[4], 71), 0),
        "mode_order": jax.random.permutation(key_of[3], MODES).astype(jnp.int32),
    }


def time_table(count):
    steps = jnp.arange(count, dtype=jnp.int32)
    half = count // 2
    freqs = jnp.arange(half, dtype=jnp.int32)
    hann = 0.5 - 0.5 * jnp.cos(2.0 * math.pi * steps.astype(jnp.float32) / count)
    phase = 2.0 * math.pi * (freqs[:, None] * steps[None, :] % count).astype(jnp.float32) / count
    factor = math.sqrt(8.0 / (3.0 * count))
    return jnp.concatenate([factor * hann[None, :] * jnp.cos(phase), -factor * hann[None, :] * jnp.sin(phase)], axis=0)

def angle_table(mode_order, angles):
    index = jnp.arange(angles, dtype=jnp.int32)
    phase = 2.0 * math.pi * (mode_order[:, None] * index[None, :] % angles).astype(jnp.float32) / angles
    cosine = jnp.cos(phase) / math.sqrt(angles)
    sine = jnp.sin(phase) / math.sqrt(angles)
    return jnp.stack([jnp.stack([cosine, sine], axis=1), jnp.stack([-sine, cosine], axis=1)], axis=0)

def reference(pressure, cell_weight, live_cells, mode_order):
    hi = lax.Precision.HIGHEST
    htab = time_table(NS)
    atab = angle_table(mode_order, THETA)

    def one_group(group):
        start = (group * GCELLS).astype(jnp.int32)
        block = lax.dynamic_slice_in_dim(pressure, start, GCELLS, 2)
        weights = lax.dynamic_slice_in_dim(cell_weight, start, GCELLS, 0)
        live = lax.dynamic_slice_in_dim(live_cells, group.astype(jnp.int32), 1, 0)[0]
        spectra = jnp.einsum('rt,tqc->rqc', htab, block, precision=hi)
        split = spectra.reshape(2, NF, THETA, GCELLS)
        modal = jnp.einsum('okiq,ifqc->kofc', atab, split, precision=hi).reshape(MODES, NS, GCELLS)
        position = jnp.arange(GCELLS, dtype=jnp.int32)
        weighted = jnp.where(position < live, weights / CELLS, jnp.float32(0.0))
        return jnp.einsum('kac,kbc->kab', modal * weighted[None, None, :], modal, precision=hi)
    parts = lax.map(one_group, jnp.arange(GROUPS, dtype=jnp.int32))
    return lax.optimization_barrier(jnp.sum(parts, axis=0))
```

```python
import functools
import math

import jax
import jax.numpy as jnp
from jax import lax
from jax.experimental import pallas as pl
from jax.experimental.pallas import tpu as pltpu
from jax.sharding import PartitionSpec as P

MESH = pl.DeviceIdType.MESH
LANES = 128
UNROLL = 4
STAGES = 4
SUB = 8
F32 = jnp.float32
BF16 = jnp.bfloat16


def halves(x):
    hi = x.astype(BF16)
    lo = (x - hi.astype(F32)).astype(BF16)
    return hi, lo


def left_terms(x):
    hi, lo = halves(x)
    return jnp.concatenate([hi, hi, lo], axis=1)


def right_terms(x):
    hi, lo = halves(x)
    return jnp.concatenate([hi, lo, hi], axis=0)


def dot(a, b, dims=(((1,), (0,)), ((), ()))):
    return lax.dot_general(a, b, dims, preferred_element_type=F32)


def partner(x, me, n):
    other, bit = 0, 1
    while bit < n:
        other += (me // bit + x // bit) % 2 * bit
        bit *= 2
    return other


def iota(shape, axis):
    return lax.broadcasted_iota(jnp.int32, shape, axis)


def time_terms(snaps):
    size = snaps * SUB
    row, col = iota((size, size), 0), iota((size, size), 1)
    half = snaps // 2
    r, t = row // SUB, col // SUB
    f = r % half
    hann = 0.5 - 0.5 * jnp.cos((2.0 * math.pi / snaps) * t.astype(F32))
    phase = (2.0 * math.pi / snaps) * ((f * t) % snaps).astype(F32)
    wave = jnp.where(r < half, jnp.cos(phase), -jnp.sin(phase))
    value = math.sqrt(8.0 / (3.0 * snaps)) * hann * wave
    return jnp.where(row % SUB == col % SUB, value, 0.0)


def angle_terms(modes_row, angles, first, count):
    index = first + iota((count, modes_row.shape[1]), 0)
    phase = (2.0 * math.pi / angles) * ((modes_row * index) % angles).astype(F32)
    scale = 1.0 / math.sqrt(angles)
    return jnp.concatenate([(jnp.cos(phase) * scale).T, (jnp.sin(phase) * scale).T], axis=0)


def kernel(n_sec, n_tile, n_role, p_ref, w_ref, live_ref, mode_ref, out_ref,
           recv, spec, zbuf, acc, pbuf, pacc, reda, sb, redb, ttab, atab, ltab, ypart,
           send_sem, recv_sem, own_sem, pa_sem, pr_sem, sa_sem, ra_sem, sb_sem, rb_sem):
    me = lax.axis_index("sec")
    tile, role = lax.axis_index("tile"), lax.axis_index("role")
    n_grp = n_tile * n_role
    grp = tile * n_role + role
    near = n_grp // 2
    side, mine = tile % 2, tile // 2 * n_role + role
    snaps, q_loc, cells = p_ref.shape
    half = snaps // 2
    angles = q_loc * n_sec
    modes = mode_ref.shape[1]
    cell_dev = cells // n_sec
    subs = cell_dev // LANES
    pack = LANES // snaps
    part = snaps // n_grp
    split = q_loc % 16 == 0

    def peer(o):
        other = lax.rem(grp + o, n_grp)
        return other, {"tile": other // n_role, "role": other % n_role}

    barrier = pltpu.get_barrier_semaphore()
    for o in range(1, n_sec):
        pl.semaphore_signal(barrier, inc=1, device_id={"sec": lax.rem(me + o, n_sec)}, device_id_type=MESH)
    for o in range(1, n_grp):
        pl.semaphore_signal(barrier, inc=1, device_id=peer(o)[1], device_id_type=MESH)
    pl.semaphore_wait(barrier, n_sec + n_grp - 2)

    def piece(owner, j):
        start = pl.multiple_of(owner * cell_dev + j * LANES, LANES)
        return p_ref.at[:, :, pl.ds(start, LANES)]

    def outgoing(i, j):
        dest = partner(i, me, n_sec)
        return pltpu.make_async_remote_copy(
            src_ref=piece(dest, j), dst_ref=recv.at[j, me],
            send_sem=send_sem.at[j, dest], recv_sem=recv_sem.at[j, me],
            device_id={"sec": dest}, device_id_type=MESH)

    def own(j):
        return pltpu.make_async_copy(piece(me, j), recv.at[j, me], own_sem.at[j])

    for j in range(subs):
        @pl.loop(1, n_sec)
        def _(i):
            outgoing(i, j).start()
    for j in range(subs):
        own(j).start()

    ttab[...] = left_terms(time_terms(snaps))
    atab[...] = left_terms(angle_terms(mode_ref[...], angles, 0, angles))
    late = partner(n_sec - 1, me, n_sec)
    late_at = pl.multiple_of(late * q_loc, SUB)
    if split:
        ltab[...] = left_terms(angle_terms(mode_ref[...], angles, late_at, q_loc))
    live = live_ref[grp]
    total = float(cells * n_grp)
    wide = 2 if q_loc % (2 * SUB) == 0 else 1

    def to_spectra(j, src):
        for g in range(0, q_loc, wide * SUB):
            x = jnp.concatenate(
                [recv[j, src, :, g + u * SUB:g + (u + 1) * SUB, :].reshape(snaps * SUB, LANES) for u in range(wide)],
                axis=1)
            y = dot(ttab[...], right_terms(x))
            for u in range(wide):
                at = pl.multiple_of(src * q_loc + g + u * SUB, SUB)
                spec[:, pl.ds(at, SUB), :] = y[:, u * LANES:(u + 1) * LANES].reshape(snaps, SUB, LANES)

    stage_rows = acc.shape[1] // STAGES

    def pair(t):
        at = pl.ds(t * stage_rows, stage_rows)
        return pltpu.make_async_remote_copy(
            src_ref=acc.at[pl.ds((1 - side) * near, near), at, :], dst_ref=pbuf.at[:, at, :],
            send_sem=pa_sem.at[t], recv_sem=pr_sem.at[t],
            device_id={"tile": tile + 1 - 2 * side}, device_id_type=MESH)

    def share(o, t, arriving=False):
        other = lax.rem(mine + o, near)
        at = pl.ds(t * stage_rows, stage_rows)
        slot = other if arriving else mine
        return pltpu.make_async_remote_copy(
            src_ref=pacc.at[other, at, :], dst_ref=reda.at[slot, at, :],
            send_sem=sa_sem.at[t, other], recv_sem=ra_sem.at[t, slot],
            device_id={"tile": other // n_role * 2 + side, "role": other % n_role}, device_id_type=MESH)

    def forward(t):
        pair(t).wait_recv()
        at = pl.ds(t * stage_rows, stage_rows)
        pacc[:, at, :] = acc[pl.ds(side * near, near), at, :] + pbuf[:, at, :]
        for o in range(1, near):
            share(o, t).start()

    def arrive(i, j):
        src = partner(i, me, n_sec)
        pltpu.make_async_remote_copy(
            src_ref=recv.at[j, src], dst_ref=recv.at[j, src],
            send_sem=send_sem.at[j, src], recv_sem=recv_sem.at[j, src],
            device_id={"sec": src}, device_id_type=MESH).wait_recv()
        to_spectra(j, src)

    def to_modal(f, y):
        zbuf[pl.ds(f, modes, stride=snaps), :] = y[:modes, :LANES] + y[modes:, LANES:]
        zbuf[pl.ds(half + f, modes, stride=snaps), :] = y[:modes, LANES:] - y[modes:, :LANES]

    def products(f):
        x = jnp.concatenate([spec[f], spec[half + f]], axis=1)
        return dot(atab[...], right_terms(x))

    for j in range(subs):
        own(j).wait()
        to_spectra(j, me)
        early = split and j == subs - 1

        @pl.loop(1, n_sec - 1 if early else n_sec)
        def _(i):
            arrive(i, j)

        if early:
            spec[:, pl.ds(late_at, q_loc), :] = jnp.zeros((snaps, q_loc, LANES), F32)

            @pl.loop(0, half)
            def _(f):
                ypart[f] = products(f)

            arrive(n_sec - 1, j)

            @pl.loop(0, half, unroll=UNROLL)
            def _(f):
                x = jnp.concatenate([spec[f, pl.ds(late_at, q_loc), :], spec[half + f, pl.ds(late_at, q_loc), :]], axis=1)
                to_modal(f, ypart[f] + dot(ltab[...], right_terms(x)))
        else:
            @pl.loop(0, half, unroll=UNROLL)
            def _(f):
                to_modal(f, products(f))

        first = pl.multiple_of(me * cell_dev + j * LANES, LANES)
        position = first + iota((1, LANES), 1)
        weight = jnp.where(position < live, w_ref[pl.ds(me * subs + j, 1), :] / total, 0.0)
        block = iota((snaps, LANES), 1) // snaps
        steps = SUB // part

        def gram(h):
            rows = []
            for u in range(steps):
                at = pl.multiple_of((h * steps + u) * LANES, LANES)
                z = zbuf[pl.ds(at, LANES), :]
                zh, zl = halves(z)
                g4 = dot(left_terms(z * weight), jnp.concatenate([zh, zl, zh], axis=1), (((1,), (1,)), ((), ())))
                r = g4[:snaps]
                for b in range(1, pack):
                    r = jnp.where(block == b, g4[b * snaps:(b + 1) * snaps], r)
                rows.append(r)
            at = pl.multiple_of(h * SUB, SUB)
            for g in range(n_grp):
                new = jnp.concatenate([r[g * part:(g + 1) * part] for r in rows], axis=0)
                to = g // n_role % 2 * near + g // n_role // 2 * n_role + g % n_role
                if j == 0:
                    acc[to, pl.ds(at, SUB), :] = new
                else:
                    acc[to, pl.ds(at, SUB), :] += new

        count = modes // pack // steps // STAGES
        for t in range(STAGES):
            pl.loop(t * count, (t + 1) * count, unroll=UNROLL)(gram)
            if j == subs - 1:
                pair(t).start()
                if t > 0:
                    forward(t - 1)

    def last(s, slot):
        return pltpu.make_async_remote_copy(
            src_ref=sb.at[s], dst_ref=redb.at[slot],
            send_sem=sb_sem.at[s], recv_sem=rb_sem.at[slot],
            device_id={"sec": s}, device_id_type=MESH)

    forward(STAGES - 1)
    rows = sb.shape[1]
    for t in range(STAGES):
        for o in range(1, near):
            share(o, t, True).wait_recv()
        for s in range(t * n_sec // STAGES, (t + 1) * n_sec // STAGES):
            value = pacc[mine, s * rows:(s + 1) * rows, :]
            for o in range(1, near):
                value += reda[lax.rem(mine + o, near), s * rows:(s + 1) * rows, :]
            sb[s] = value

            @pl.when(me != s)
            def _():
                last(s, me).start()

    value = sb[me]
    for o in range(1, n_sec):
        s = lax.rem(me + o, n_sec)
        last(s, s).wait_recv()
        value += redb[s]
    out_ref[...] = value

    for j in range(subs):
        @pl.loop(1, n_sec)
        def _(i):
            outgoing(i, j).wait_send()
    for t in range(STAGES):
        pair(t).wait_send()
        for o in range(1, near):
            share(o, t).wait_send()
    for o in range(1, n_sec):
        last(lax.rem(me + o, n_sec), me).wait_send()


def flip(x, bit):
    return x + bit - 2 * bit * (x // bit % 2)


def slot_table(slots, n_sec, subs):
    half = n_sec // 2
    table = [None] * slots
    for right in (1, 0):
        mine = range(1 - right, slots, 2)
        pad = subs * half - len(mine)
        for i, j in enumerate(mine):
            at = half - 1 - (i + pad) % half
            table[j] = (half + at if right else half - 1 - at, (i + pad) // half)
    return table


def ragged(slots, floor, n_sec, n_tile, n_role, *refs):
    n_grp = n_tile * n_role
    near = n_grp // 2
    (p_ref, w_ref, live_ref, mode_ref, out_ref,
     recv, spec, zbuf, acc, pbuf, pacc, reda, sb, redb, ttab, atab, ltab, ypart,
     send_sem, recv_sem, own_sem, pa_sem, pr_sem, sa_sem, ra_sem, sb_sem, rb_sem) = refs[:27]
    extra = refs[27:]
    me = lax.axis_index("sec")
    tile, role = lax.axis_index("tile"), lax.axis_index("role")
    grp = tile * n_role + role
    side, mine = tile % 2, tile // 2 * n_role + role
    snaps, q_loc, cells = p_ref.shape
    half = snaps // 2
    angles = q_loc * n_sec
    modes = mode_ref.shape[1]
    blocks = cells // LANES
    subs = recv.shape[0]
    pack = LANES // snaps
    part = snaps // n_grp
    spare = blocks - slots
    fixed = floor if spare else slots
    table = slot_table(slots, n_sec, subs)
    core, xbit, ybit = n_role, 1, 2 * n_role
    if spare:
        pools, stage, wall, home_sem, keep_sem, ls_sem, lr_sem, ws_sem, wr_sem = (
            extra[:spare], *extra[spare:])

    def at_plane(g):
        return {"tile": g // n_role, "role": g % n_role}

    barrier = pltpu.get_barrier_semaphore()
    for o in range(1, n_sec):
        pl.semaphore_signal(barrier, inc=1, device_id={"sec": lax.rem(me + o, n_sec)}, device_id_type=MESH)
    for o in range(1, n_grp):
        pl.semaphore_signal(barrier, inc=1, device_id=at_plane(lax.rem(grp + o, n_grp)), device_id_type=MESH)
    pl.semaphore_wait(barrier, n_sec + n_grp - 2)

    def piece(j):
        return p_ref.at[:, :, pl.ds(j * LANES, LANES)]

    def content(j):
        return piece(j) if j < fixed else stage.at[j - fixed]

    def owner(j):
        z = table[j][0]
        return z + side * (n_sec - 1 - 2 * z)

    def outgoing(j):
        sub = table[j][1]
        return pltpu.make_async_remote_copy(
            src_ref=content(j), dst_ref=recv.at[sub, me],
            send_sem=send_sem.at[j], recv_sem=recv_sem.at[sub, me],
            device_id={"sec": owner(j)}, device_id_type=MESH)

    def own(j):
        sub = table[j][1]
        return pltpu.make_async_copy(content(j), recv.at[sub, me], own_sem.at[sub])

    def is_far(j):
        return owner(j) // (n_sec // 2) != me // (n_sec // 2)

    def launch(js):
        for j in js:
            @pl.when(is_far(j))
            def _():
                outgoing(j).start()
        for j in js:
            @pl.when(jnp.logical_and(jnp.logical_not(is_far(j)), owner(j) != me))
            def _():
                outgoing(j).start()

            @pl.when(owner(j) == me)
            def _():
                own(j).start()

    launch(range(fixed))

    count = [jnp.maximum((live_ref[g] + (LANES - 1)) // LANES, fixed) for g in range(n_grp)]

    def plan(j):
        mine_count = jnp.int32(0)
        want = jnp.int32(0)
        for g in range(n_grp):
            mine_count += jnp.where(grp == g, count[g], 0)
            for k in range(fixed, slots):
                want += jnp.where(jnp.logical_and(k < j, count[g] <= k), 1, 0)
            want += jnp.where(jnp.logical_and(g < grp, count[g] <= j), 1, 0)
        home = j < mine_count
        seen = jnp.int32(0)
        from_g, from_k, found = jnp.int32(0), jnp.int32(0), jnp.int32(0)
        for k in range(spare):
            for g in range(n_grp):
                has = jnp.where(count[g] > slots + k, 1, 0)
                hit = jnp.where(seen == want, has, 0)
                from_g += hit * g
                from_k += hit * k
                found += hit
                seen += has
        return home, found, from_g, from_k

    if spare:
        gx, gy, gc = flip(grp, xbit), flip(grp, ybit), flip(grp, core)
        gxy = flip(gx, ybit)
        offset = slots - fixed

        def place(k, g):
            return pools[k].at[g + (offset if k == 0 else 0)]

        def pass_on(k, n, origin, to):
            src = piece(slots + k) if origin is grp else place(k, origin)
            return pltpu.make_async_remote_copy(
                src_ref=src, dst_ref=place(k, origin),
                send_sem=ls_sem.at[k, n], recv_sem=lr_sem.at[k, origin],
                device_id=at_plane(to), device_id_type=MESH)

        hops = [(grp, gx), (grp, gy), (grp, gc), (gx, gy), (gx, gc), (gy, gc), (gxy, gc)]

        def hop(k, n):
            return pass_on(k, n, *hops[n])

        def came(k, origin):
            pltpu.make_async_remote_copy(
                src_ref=place(k, origin), dst_ref=place(k, origin),
                send_sem=ls_sem.at[k, 0], recv_sem=lr_sem.at[k, origin],
                device_id=at_plane(gx), device_id_type=MESH).wait_recv()

        def keep(k):
            return pltpu.make_async_copy(piece(slots + k), place(k, grp), keep_sem.at[k])

        def hold(j):
            return pltpu.make_async_copy(piece(j), pools[0].at[j - fixed], home_sem.at[j - fixed])

        def weight_to(o):
            return pltpu.make_async_remote_copy(
                src_ref=w_ref, dst_ref=wall.at[grp],
                send_sem=ws_sem.at[o], recv_sem=wr_sem.at[grp],
                device_id=at_plane(lax.rem(grp + o, n_grp)), device_id_type=MESH)

        def weight_from(o):
            other = lax.rem(grp + o, n_grp)
            return pltpu.make_async_remote_copy(
                src_ref=w_ref, dst_ref=wall.at[other],
                send_sem=ws_sem.at[o], recv_sem=wr_sem.at[other],
                device_id=at_plane(other), device_id_type=MESH)

        for k in range(spare):
            for n in (0, 1, 2) if k == 0 else (0, 2):
                hop(k, n).start()
        for j in range(fixed, slots):
            hold(j).start()
        for k in range(spare):
            keep(k).start()
        for o in range(1, n_grp):
            weight_to(o).start()
        wall[grp] = w_ref[...]

    acc[...] = jnp.zeros(acc.shape, F32)
    ttab[...] = left_terms(time_terms(snaps))
    atab[...] = left_terms(angle_terms(mode_ref[...], angles, 0, angles))
    late = partner(n_sec - 1, me, n_sec)
    late_at = pl.multiple_of(late * q_loc, SUB)
    ltab[...] = left_terms(angle_terms(mode_ref[...], angles, late_at, q_loc))
    total = float(cells * n_grp)

    if spare:
        def fill(j):
            home, found, from_g, from_k = plan(j)
            foreign = jnp.where(home, 0, found)
            first = jnp.where(jnp.logical_and(foreign == 1, from_k == 0), from_g + offset, j - fixed)
            second = jnp.where(jnp.logical_and(foreign == 1, from_k == 1), 1, 0)
            both = spare > 1 and j > fixed

            @pl.loop(0, snaps, unroll=UNROLL)
            def _(t):
                x = pools[0][first, t]
                if both:
                    x = jnp.where(second == 1, pools[1][from_g, t], x)
                stage[j - fixed, t] = x

        for k in range(spare):
            came(k, gx)
            hop(k, 3).start()
            hop(k, 4).start()
            if k + 1 < spare:
                hop(k + 1, 1).start()
            came(k, gy)
            hop(k, 5).start()
            came(k, gxy)
            hop(k, 6).start()
            for g in (gc, flip(gx, core), flip(gy, core), flip(gxy, core)):
                came(k, g)
            keep(k).wait()
            if k == 0:
                for j in range(fixed, slots):
                    hold(j).wait()
            js = range(fixed, slots) if spare == 1 else (range(fixed, fixed + 1) if k == 0 else range(fixed + 1, slots))
            for j in js:
                fill(j)
                launch([j])
        for o in range(1, n_grp):
            weight_from(o).wait_recv()

    rank = me + side * (n_sec - 1 - 2 * me)

    def holding(sub):
        slot, have = jnp.int32(0), jnp.int32(0)
        for j, (z, s) in enumerate(table):
            if s == sub:
                slot += jnp.where(rank == z, j, 0)
                have += jnp.where(rank == z, 1, 0)
        return slot, have

    def weight_row(sub):
        slot, _ = holding(sub)
        lane = iota((1, LANES), 1)
        row = iota((blocks, LANES), 0)
        if spare:
            home, found, from_g, from_k = plan(slot)
            g = jnp.where(home, grp, from_g)
            b = jnp.where(home, slot, slots + from_k)
            used = jnp.where(home, 1, found)
            live = jnp.int32(0)
            w = jnp.zeros((1, LANES), F32)
            for h in range(n_grp):
                live += jnp.where(g == h, live_ref[h], 0)
                w += jnp.sum(jnp.where(row == jnp.where(g == h, b, -1), wall[h], 0.0), axis=0, keepdims=True)
            live = jnp.where(used == 1, live, 0)
        else:
            b, live = slot, live_ref[grp]
            w = jnp.sum(jnp.where(row == b, w_ref[...], 0.0), axis=0, keepdims=True)
        return jnp.where(b * LANES + lane < live, w / total, 0.0)

    wide = 2

    def to_spectra(j, src):
        for g in range(0, q_loc, wide * SUB):
            x = jnp.concatenate(
                [recv[j, src, :, g + u * SUB:g + (u + 1) * SUB, :].reshape(snaps * SUB, LANES) for u in range(wide)],
                axis=1)
            y = dot(ttab[...], right_terms(x))
            for u in range(wide):
                at = pl.multiple_of(src * q_loc + g + u * SUB, SUB)
                spec[:, pl.ds(at, SUB), :] = y[:, u * LANES:(u + 1) * LANES].reshape(snaps, SUB, LANES)

    stage_rows = acc.shape[1] // STAGES

    def pair(t):
        at = pl.ds(t * stage_rows, stage_rows)
        return pltpu.make_async_remote_copy(
            src_ref=acc.at[pl.ds((1 - side) * near, near), at, :], dst_ref=pbuf.at[:, at, :],
            send_sem=pa_sem.at[t], recv_sem=pr_sem.at[t],
            device_id={"tile": tile + 1 - 2 * side}, device_id_type=MESH)

    def share(o, t, arriving=False):
        other = lax.rem(mine + o, near)
        at = pl.ds(t * stage_rows, stage_rows)
        slot = other if arriving else mine
        return pltpu.make_async_remote_copy(
            src_ref=pacc.at[other, at, :], dst_ref=reda.at[slot, at, :],
            send_sem=sa_sem.at[t, other], recv_sem=ra_sem.at[t, slot],
            device_id={"tile": other // n_role * 2 + side, "role": other % n_role}, device_id_type=MESH)

    def forward(t):
        pair(t).wait_recv()
        at = pl.ds(t * stage_rows, stage_rows)
        pacc[:, at, :] = acc[pl.ds(side * near, near), at, :] + pbuf[:, at, :]
        for o in range(1, near):
            share(o, t).start()

    def arrive(i, j):
        src = partner(i, me, n_sec)
        pltpu.make_async_remote_copy(
            src_ref=recv.at[j, src], dst_ref=recv.at[j, src],
            send_sem=send_sem.at[j], recv_sem=recv_sem.at[j, src],
            device_id={"sec": src}, device_id_type=MESH).wait_recv()
        to_spectra(j, src)

    def to_modal(f, y):
        zbuf[pl.ds(f, modes, stride=snaps), :] = y[:modes, :LANES] + y[modes:, LANES:]
        zbuf[pl.ds(half + f, modes, stride=snaps), :] = y[:modes, LANES:] - y[modes:, :LANES]

    def products(f):
        x = jnp.concatenate([spec[f], spec[half + f]], axis=1)
        return dot(atab[...], right_terms(x))

    def process(j):
        early = j == subs - 1
        pltpu.make_async_copy(piece(0), recv.at[j, me], own_sem.at[j]).wait()
        to_spectra(j, me)

        @pl.loop(1, n_sec - 1 if early else n_sec)
        def _(i):
            arrive(i, j)

        if early:
            spec[:, pl.ds(late_at, q_loc), :] = jnp.zeros((snaps, q_loc, LANES), F32)

            @pl.loop(0, half)
            def _(f):
                ypart[f] = products(f)

            arrive(n_sec - 1, j)

            @pl.loop(0, half, unroll=UNROLL)
            def _(f):
                x = jnp.concatenate([spec[f, pl.ds(late_at, q_loc), :], spec[half + f, pl.ds(late_at, q_loc), :]], axis=1)
                to_modal(f, ypart[f] + dot(ltab[...], right_terms(x)))
        else:
            @pl.loop(0, half, unroll=UNROLL)
            def _(f):
                to_modal(f, products(f))

        weight = weight_row(j)
        block = iota((snaps, LANES), 1) // snaps
        steps = SUB // part

        def gram(h):
            rows = []
            for u in range(steps):
                at = pl.multiple_of((h * steps + u) * LANES, LANES)
                z = zbuf[pl.ds(at, LANES), :]
                zh, zl = halves(z)
                g4 = dot(left_terms(z * weight), jnp.concatenate([zh, zl, zh], axis=1), (((1,), (1,)), ((), ())))
                r = g4[:snaps]
                for b in range(1, pack):
                    r = jnp.where(block == b, g4[b * snaps:(b + 1) * snaps], r)
                rows.append(r)
            at = pl.multiple_of(h * SUB, SUB)
            for g in range(n_grp):
                new = jnp.concatenate([r[g * part:(g + 1) * part] for r in rows], axis=0)
                to = g // n_role % 2 * near + g // n_role // 2 * n_role + g % n_role
                acc[to, pl.ds(at, SUB), :] += new

        size = modes // pack // steps // STAGES
        for t in range(STAGES):
            pl.loop(t * size, (t + 1) * size, unroll=UNROLL)(gram)
            if early:
                pair(t).start()
                if t > 0:
                    forward(t - 1)

    for j in range(subs - 1):
        pl.when(holding(j)[1] == 1)(functools.partial(process, j))
    process(subs - 1)

    def last(s, slot):
        return pltpu.make_async_remote_copy(
            src_ref=sb.at[s], dst_ref=redb.at[slot],
            send_sem=sb_sem.at[s], recv_sem=rb_sem.at[slot],
            device_id={"sec": s}, device_id_type=MESH)

    forward(STAGES - 1)
    rows = sb.shape[1]
    for t in range(STAGES):
        for o in range(1, near):
            share(o, t, True).wait_recv()
        for s in range(t * n_sec // STAGES, (t + 1) * n_sec // STAGES):
            value = pacc[mine, s * rows:(s + 1) * rows, :]
            for o in range(1, near):
                value += reda[lax.rem(mine + o, near), s * rows:(s + 1) * rows, :]
            sb[s] = value

            @pl.when(me != s)
            def _():
                last(s, me).start()

    value = sb[me]
    for o in range(1, n_sec):
        s = lax.rem(me + o, n_sec)
        last(s, s).wait_recv()
        value += redb[s]
    out_ref[...] = value

    for j in range(slots):
        @pl.when(owner(j) != me)
        def _():
            outgoing(j).wait_send()
    if spare:
        for k in range(spare):
            for n in range(len(hops)):
                hop(k, n).wait_send()
        for o in range(1, n_grp):
            weight_to(o).wait_send()
    for t in range(STAGES):
        pair(t).wait_send()
        for o in range(1, near):
            share(o, t).wait_send()
    for o in range(1, n_sec):
        last(lax.rem(me + o, n_sec), me).wait_send()


def on_device(pressure, cell_weight, live_cells, mode_order):
    n_sec, n_tile, n_role = (lax.axis_size(a) for a in ("sec", "tile", "role"))
    n_grp = n_tile * n_role
    snaps, q_loc, cells = pressure.shape
    modes = mode_order.shape[0]
    angles = q_loc * n_sec
    blocks = cells // LANES
    subs = blocks // n_sec
    pack = LANES // snaps
    part = snaps // n_grp
    rows = modes // pack * part
    own_rows = rows // n_sec
    vmem = pl.BlockSpec(memory_space=pltpu.VMEM)
    dma = pltpu.SemaphoreType.DMA
    adaptive = subs == 2 and n_grp == blocks and n_role == 2 and n_sec == 4 and q_loc % 16 == 0
    floor = -(-(cells // 3) // LANES)

    def scratch(slots):
        shapes = [
            pltpu.VMEM((subs, n_sec, snaps, q_loc, LANES), F32),
            pltpu.VMEM((snaps, angles, LANES), F32),
            pltpu.VMEM((modes * snaps, LANES), F32),
            pltpu.VMEM((n_grp, rows, LANES), F32),
            pltpu.VMEM((n_grp // 2, rows, LANES), F32),
            pltpu.VMEM((n_grp // 2, rows, LANES), F32),
            pltpu.VMEM((n_grp // 2, rows, LANES), F32),
            pltpu.VMEM((n_sec, own_rows, LANES), F32),
            pltpu.VMEM((n_sec, own_rows, LANES), F32),
            pltpu.VMEM((snaps * SUB, 3 * snaps * SUB), BF16),
            pltpu.VMEM((2 * modes, 3 * angles), BF16),
            pltpu.VMEM((2 * modes, 3 * q_loc), BF16),
            pltpu.VMEM((snaps // 2, 2 * modes, 2 * LANES), F32),
            dma((slots,) if adaptive else (subs, n_sec)), dma((subs, n_sec)), dma((subs,)),
            dma((STAGES,)), dma((STAGES,)), dma((STAGES, n_grp // 2)), dma((STAGES, n_grp // 2)), dma((n_sec,)), dma((n_sec,)),
        ]
        spare = blocks - slots
        if adaptive and spare:
            block = (snaps, q_loc, LANES)
            extra = slots - floor
            shapes += [pltpu.VMEM((n_grp + (extra if k == 0 else 0), *block), F32) for k in range(spare)]
            shapes += [
                pltpu.VMEM((extra, *block), F32),
                pltpu.VMEM((n_grp, blocks, LANES), F32),
                dma((extra,)), dma((spare,)), dma((spare, n_grp)), dma((spare, n_grp)), dma((n_grp,)), dma((n_grp,)),
            ]
        return shapes

    def call(slots):
        body = functools.partial(ragged, slots, floor) if adaptive else kernel
        return pl.pallas_call(
            functools.partial(body, n_sec, n_tile, n_role),
            out_shape=jax.ShapeDtypeStruct((own_rows, LANES), F32),
            in_specs=[pl.BlockSpec(memory_space=pl.ANY), vmem, pl.BlockSpec(memory_space=pltpu.SMEM), vmem],
            out_specs=vmem,
            scratch_shapes=scratch(slots),
            compiler_params=pltpu.CompilerParams(
                collective_id=blocks - slots, has_side_effects=True, vmem_limit_bytes=62 * 2**20),
            name="spod",
        )

    args = (pressure, cell_weight.reshape(blocks, LANES), live_cells, mode_order.reshape(1, modes))
    if adaptive:
        count = jnp.maximum((live_cells + (LANES - 1)) // LANES, floor)
        low = blocks - 2
        code = jnp.sum(count + 256 * (count <= floor) + 4096 * (count > low) + 65536 * (count > low + 1))
        total, short = code % 256, code // 256 % 16
        over, more = code // 4096 % 16, code // 65536
        tight = jnp.logical_and(total <= low * n_grp, jnp.logical_or(short <= over, more == 0))
        pick = jnp.where(tight, 2, jnp.where(total <= (low + 1) * n_grp, 1, 0))
        packed = lax.switch(pick, [call(blocks), call(blocks - 1), call(blocks - 2)], *args)
    else:
        packed = call(blocks)(*args)
    out = packed.reshape(modes // pack // n_sec, part, pack, snaps)
    return out.transpose(0, 2, 1, 3).reshape(modes // n_sec, part, snaps)


def solution(mesh):
    in_specs = (P(None, "sec", ("tile", "role")), P(("tile", "role")), P(), P())
    out_specs = P("sec", ("tile", "role"), None)
    return jax.shard_map(
        on_device, mesh=mesh, in_specs=in_specs, out_specs=out_specs, check_vma=False
    )
```

```python
import functools
import math

import jax
import jax.numpy as jnp
from jax import lax
from jax.experimental import pallas as pl
from jax.experimental.pallas import tpu as pltpu
from jax.sharding import PartitionSpec as P

MESH = pl.DeviceIdType.MESH
LANES = 128
UNROLL = 4
STAGES = 4
SUB = 8
F32 = jnp.float32
BF16 = jnp.bfloat16


def halves(x):
    hi = x.astype(BF16)
    lo = (x - hi.astype(F32)).astype(BF16)
    return hi, lo


def left_terms(x):
    hi, lo = halves(x)
    return jnp.concatenate([hi, hi, lo], axis=1)


def right_terms(x):
    hi, lo = halves(x)
    return jnp.concatenate([hi, lo, hi], axis=0)


def dot(a, b, dims=(((1,), (0,)), ((), ()))):
    return lax.dot_general(a, b, dims, preferred_element_type=F32)


def partner(x, me, n):
    other, bit = 0, 1
    while bit < n:
        other += (me // bit + x // bit) % 2 * bit
        bit *= 2
    return other


def iota(shape, axis):
    return lax.broadcasted_iota(jnp.int32, shape, axis)


def time_terms(snaps):
    size = snaps * SUB
    row, col = iota((size, size), 0), iota((size, size), 1)
    half = snaps // 2
    r, t = row // SUB, col // SUB
    f = r % half
    hann = 0.5 - 0.5 * jnp.cos((2.0 * math.pi / snaps) * t.astype(F32))
    phase = (2.0 * math.pi / snaps) * ((f * t) % snaps).astype(F32)
    wave = jnp.where(r < half, jnp.cos(phase), -jnp.sin(phase))
    value = math.sqrt(8.0 / (3.0 * snaps)) * hann * wave
    return jnp.where(row % SUB == col % SUB, value, 0.0)


def angle_terms(modes_row, angles, first, count):
    index = first + iota((count, modes_row.shape[1]), 0)
    phase = (2.0 * math.pi / angles) * ((modes_row * index) % angles).astype(F32)
    scale = 1.0 / math.sqrt(angles)
    return jnp.concatenate([(jnp.cos(phase) * scale).T, (jnp.sin(phase) * scale).T], axis=0)


def kernel(n_sec, n_tile, n_role, p_ref, w_ref, live_ref, mode_ref, out_ref,
           recv, spec, zbuf, acc, pbuf, pacc, reda, sb, redb, ttab, atab, ltab, ypart,
           send_sem, recv_sem, own_sem, pa_sem, pr_sem, sa_sem, ra_sem, sb_sem, rb_sem):
    me = lax.axis_index("sec")
    tile, role = lax.axis_index("tile"), lax.axis_index("role")
    n_grp = n_tile * n_role
    grp = tile * n_role + role
    near = n_grp // 2
    side, mine = tile % 2, tile // 2 * n_role + role
    snaps, q_loc, cells = p_ref.shape
    half = snaps // 2
    angles = q_loc * n_sec
    modes = mode_ref.shape[1]
    cell_dev = cells // n_sec
    subs = cell_dev // LANES
    pack = LANES // snaps
    part = snaps // n_grp
    split = q_loc % 16 == 0

    def peer(o):
        other = lax.rem(grp + o, n_grp)
        return other, {"tile": other // n_role, "role": other % n_role}

    barrier = pltpu.get_barrier_semaphore()
    for o in range(1, n_sec):
        pl.semaphore_signal(barrier, inc=1, device_id={"sec": lax.rem(me + o, n_sec)}, device_id_type=MESH)
    for o in range(1, n_grp):
        pl.semaphore_signal(barrier, inc=1, device_id=peer(o)[1], device_id_type=MESH)
    pl.semaphore_wait(barrier, n_sec + n_grp - 2)

    def piece(owner, j):
        start = pl.multiple_of(owner * cell_dev + j * LANES, LANES)
        return p_ref.at[:, :, pl.ds(start, LANES)]

    def outgoing(i, j):
        dest = partner(i, me, n_sec)
        return pltpu.make_async_remote_copy(
            src_ref=piece(dest, j), dst_ref=recv.at[j, me],
            send_sem=send_sem.at[j, dest], recv_sem=recv_sem.at[j, me],
            device_id={"sec": dest}, device_id_type=MESH)

    def own(j):
        return pltpu.make_async_copy(piece(me, j), recv.at[j, me], own_sem.at[j])

    for j in range(subs):
        @pl.loop(1, n_sec)
        def _(i):
            outgoing(i, j).start()
    for j in range(subs):
        own(j).start()

    ttab[...] = left_terms(time_terms(snaps))
    atab[...] = left_terms(angle_terms(mode_ref[...], angles, 0, angles))
    late = partner(n_sec - 1, me, n_sec)
    late_at = pl.multiple_of(late * q_loc, SUB)
    if split:
        ltab[...] = left_terms(angle_terms(mode_ref[...], angles, late_at, q_loc))
    live = live_ref[grp]
    total = float(cells * n_grp)
    wide = 2 if q_loc % (2 * SUB) == 0 else 1

    def to_spectra(j, src):
        for g in range(0, q_loc, wide * SUB):
            x = jnp.concatenate(
                [recv[j, src, :, g + u * SUB:g + (u + 1) * SUB, :].reshape(snaps * SUB, LANES) for u in range(wide)],
                axis=1)
            y = dot(ttab[...], right_terms(x))
            for u in range(wide):
                at = pl.multiple_of(src * q_loc + g + u * SUB, SUB)
                spec[:, pl.ds(at, SUB), :] = y[:, u * LANES:(u + 1) * LANES].reshape(snaps, SUB, LANES)

    stage_rows = acc.shape[1] // STAGES

    def pair(t):
        at = pl.ds(t * stage_rows, stage_rows)
        return pltpu.make_async_remote_copy(
            src_ref=acc.at[pl.ds((1 - side) * near, near), at, :], dst_ref=pbuf.at[:, at, :],
            send_sem=pa_sem.at[t], recv_sem=pr_sem.at[t],
            device_id={"tile": tile + 1 - 2 * side}, device_id_type=MESH)

    def share(o, t, arriving=False):
        other = lax.rem(mine + o, near)
        at = pl.ds(t * stage_rows, stage_rows)
        slot = other if arriving else mine
        return pltpu.make_async_remote_copy(
            src_ref=pacc.at[other, at, :], dst_ref=reda.at[slot, at, :],
            send_sem=sa_sem.at[t, other], recv_sem=ra_sem.at[t, slot],
            device_id={"tile": other // n_role * 2 + side, "role": other % n_role}, device_id_type=MESH)

    def forward(t):
        pair(t).wait_recv()
        at = pl.ds(t * stage_rows, stage_rows)
        pacc[:, at, :] = acc[pl.ds(side * near, near), at, :] + pbuf[:, at, :]
        for o in range(1, near):
            share(o, t).start()

    def arrive(i, j):
        src = partner(i, me, n_sec)
        pltpu.make_async_remote_copy(
            src_ref=recv.at[j, src], dst_ref=recv.at[j, src],
            send_sem=send_sem.at[j, src], recv_sem=recv_sem.at[j, src],
            device_id={"sec": src}, device_id_type=MESH).wait_recv()
        to_spectra(j, src)

    def to_modal(f, y):
        zbuf[pl.ds(f, modes, stride=snaps), :] = y[:modes, :LANES] + y[modes:, LANES:]
        zbuf[pl.ds(half + f, modes, stride=snaps), :] = y[:modes, LANES:] - y[modes:, :LANES]

    def products(f):
        x = jnp.concatenate([spec[f], spec[half + f]], axis=1)
        return dot(atab[...], right_terms(x))

    for j in range(subs):
        own(j).wait()
        to_spectra(j, me)
        early = split and j == subs - 1

        @pl.loop(1, n_sec - 1 if early else n_sec)
        def _(i):
            arrive(i, j)

        if early:
            spec[:, pl.ds(late_at, q_loc), :] = jnp.zeros((snaps, q_loc, LANES), F32)

            @pl.loop(0, half)
            def _(f):
                ypart[f] = products(f)

            arrive(n_sec - 1, j)

            @pl.loop(0, half, unroll=UNROLL)
            def _(f):
                x = jnp.concatenate([spec[f, pl.ds(late_at, q_loc), :], spec[half + f, pl.ds(late_at, q_loc), :]], axis=1)
                to_modal(f, ypart[f] + dot(ltab[...], right_terms(x)))
        else:
            @pl.loop(0, half, unroll=UNROLL)
            def _(f):
                to_modal(f, products(f))

        first = pl.multiple_of(me * cell_dev + j * LANES, LANES)
        position = first + iota((1, LANES), 1)
        weight = jnp.where(position < live, w_ref[pl.ds(me * subs + j, 1), :] / total, 0.0)
        block = iota((snaps, LANES), 1) // snaps
        steps = SUB // part

        def gram(h):
            rows = []
            for u in range(steps):
                at = pl.multiple_of((h * steps + u) * LANES, LANES)
                z = zbuf[pl.ds(at, LANES), :]
                zh, zl = halves(z)
                g4 = dot(left_terms(z * weight), jnp.concatenate([zh, zl, zh], axis=1), (((1,), (1,)), ((), ())))
                r = g4[:snaps]
                for b in range(1, pack):
                    r = jnp.where(block == b, g4[b * snaps:(b + 1) * snaps], r)
                rows.append(r)
            at = pl.multiple_of(h * SUB, SUB)
            for g in range(n_grp):
                new = jnp.concatenate([r[g * part:(g + 1) * part] for r in rows], axis=0)
                to = g // n_role % 2 * near + g // n_role // 2 * n_role + g % n_role
                if j == 0:
                    acc[to, pl.ds(at, SUB), :] = new
                else:
                    acc[to, pl.ds(at, SUB), :] += new

        count = modes // pack // steps // STAGES
        for t in range(STAGES):
            pl.loop(t * count, (t + 1) * count, unroll=UNROLL)(gram)
            if j == subs - 1:
                pair(t).start()
                if t > 0:
                    forward(t - 1)

    def last(s, slot):
        return pltpu.make_async_remote_copy(
            src_ref=sb.at[s], dst_ref=redb.at[slot],
            send_sem=sb_sem.at[s], recv_sem=rb_sem.at[slot],
            device_id={"sec": s}, device_id_type=MESH)

    forward(STAGES - 1)
    rows = sb.shape[1]
    for t in range(STAGES):
        for o in range(1, near):
            share(o, t, True).wait_recv()
        for s in range(t * n_sec // STAGES, (t + 1) * n_sec // STAGES):
            value = pacc[mine, s * rows:(s + 1) * rows, :]
            for o in range(1, near):
                value += reda[lax.rem(mine + o, near), s * rows:(s + 1) * rows, :]
            sb[s] = value

            @pl.when(me != s)
            def _():
                last(s, me).start()

    value = sb[me]
    for o in range(1, n_sec):
        s = lax.rem(me + o, n_sec)
        last(s, s).wait_recv()
        value += redb[s]
    out_ref[...] = value

    for j in range(subs):
        @pl.loop(1, n_sec)
        def _(i):
            outgoing(i, j).wait_send()
    for t in range(STAGES):
        pair(t).wait_send()
        for o in range(1, near):
            share(o, t).wait_send()
    for o in range(1, n_sec):
        last(lax.rem(me + o, n_sec), me).wait_send()


def flip(x, bit):
    return x + bit - 2 * bit * (x // bit % 2)


def slot_table(slots, n_sec, subs):
    half = n_sec // 2
    table = [None] * slots
    for right in (1, 0):
        mine = range(1 - right, slots, 2)
        pad = subs * half - len(mine)
        for i, j in enumerate(mine):
            at = half - 1 - (i + pad) % half
            table[j] = (half + at if right else half - 1 - at, (i + pad) // half)
    return table


def ragged(slots, floor, n_sec, n_tile, n_role, *refs):
    n_grp = n_tile * n_role
    near = n_grp // 2
    (p_ref, w_ref, live_ref, mode_ref, out_ref,
     recv, spec, zbuf, acc, pbuf, pacc, reda, sb, redb, ttab, atab, ltab, ypart,
     send_sem, recv_sem, own_sem, pa_sem, pr_sem, sa_sem, ra_sem, sb_sem, rb_sem) = refs[:27]
    extra = refs[27:]
    me = lax.axis_index("sec")
    tile, role = lax.axis_index("tile"), lax.axis_index("role")
    grp = tile * n_role + role
    side, mine = tile % 2, tile // 2 * n_role + role
    snaps, q_loc, cells = p_ref.shape
    half = snaps // 2
    angles = q_loc * n_sec
    modes = mode_ref.shape[1]
    blocks = cells // LANES
    subs = recv.shape[0]
    pack = LANES // snaps
    part = snaps // n_grp
    spare = blocks - slots
    fixed = floor if spare else slots
    table = slot_table(slots, n_sec, subs)
    core, xbit, ybit = n_role, 1, 2 * n_role
    if spare:
        pools, stage, wall, home_sem, keep_sem, ls_sem, lr_sem, lt_sem, ws_sem, wr_sem = (
            extra[:spare], *extra[spare:])

    def at_plane(g):
        return {"tile": g // n_role, "role": g % n_role}

    barrier = pltpu.get_barrier_semaphore()
    for o in range(1, n_sec):
        pl.semaphore_signal(barrier, inc=1, device_id={"sec": lax.rem(me + o, n_sec)}, device_id_type=MESH)
    for o in range(1, n_grp):
        pl.semaphore_signal(barrier, inc=1, device_id=at_plane(lax.rem(grp + o, n_grp)), device_id_type=MESH)
    pl.semaphore_wait(barrier, n_sec + n_grp - 2)

    def piece(j):
        return p_ref.at[:, :, pl.ds(j * LANES, LANES)]

    def content(j):
        return piece(j) if j < fixed else stage.at[j - fixed]

    def owner(j):
        z = table[j][0]
        return z + side * (n_sec - 1 - 2 * z)

    def outgoing(j):
        sub = table[j][1]
        return pltpu.make_async_remote_copy(
            src_ref=content(j), dst_ref=recv.at[sub, me],
            send_sem=send_sem.at[j], recv_sem=recv_sem.at[sub, me],
            device_id={"sec": owner(j)}, device_id_type=MESH)

    def own(j):
        sub = table[j][1]
        return pltpu.make_async_copy(content(j), recv.at[sub, me], own_sem.at[sub])

    def is_far(j):
        return owner(j) // (n_sec // 2) != me // (n_sec // 2)

    def launch(js):
        for j in js:
            @pl.when(is_far(j))
            def _():
                outgoing(j).start()
        for j in js:
            @pl.when(jnp.logical_and(jnp.logical_not(is_far(j)), owner(j) != me))
            def _():
                outgoing(j).start()

            @pl.when(owner(j) == me)
            def _():
                own(j).start()

    launch(range(fixed))

    count = [jnp.maximum((live_ref[g] + (LANES - 1)) // LANES, fixed) for g in range(n_grp)]

    def plan(j):
        mine_count = jnp.int32(0)
        want = jnp.int32(0)
        for g in range(n_grp):
            mine_count += jnp.where(grp == g, count[g], 0)
            for k in range(fixed, slots):
                want += jnp.where(jnp.logical_and(k < j, count[g] <= k), 1, 0)
            want += jnp.where(jnp.logical_and(g < grp, count[g] <= j), 1, 0)
        home = j < mine_count
        seen = jnp.int32(0)
        from_g, from_k, found = jnp.int32(0), jnp.int32(0), jnp.int32(0)
        for k in range(spare):
            for g in range(n_grp):
                has = jnp.where(count[g] > slots + k, 1, 0)
                hit = jnp.where(seen == want, has, 0)
                from_g += hit * g
                from_k += hit * k
                found += hit
                seen += has
        return home, found, from_g, from_k

    if spare:
        gx, gy, gc = flip(grp, xbit), flip(grp, ybit), flip(grp, core)
        gxy = flip(gx, ybit)
        offset = slots - fixed

        def place(k, g):
            return pools[k].at[g + (offset if k == 0 else 0)]

        middle = snaps // 2
        bottom, top = pl.ds(0, middle), pl.ds(middle, middle)
        hops = [(grp, gx, None), (grp, gy, None), (grp, gc, None), (gx, gy, bottom), (gy, gx, top),
                (gx, gc, None), (gy, gc, None), (gxy, gc, None)]

        def hop(k, n):
            origin, to, at = hops[n]
            src = piece(slots + k) if n < 3 else place(k, origin)
            dst = place(k, origin)
            if at is not None:
                src, dst = src.at[at], dst.at[at]
            arrival = lr_sem.at[k, origin] if at is not top else lt_sem.at[k]
            return pltpu.make_async_remote_copy(
                src_ref=src, dst_ref=dst, send_sem=ls_sem.at[k, n], recv_sem=arrival,
                device_id=at_plane(to), device_id_type=MESH)

        def came(k, origin, at=None):
            dst = place(k, origin)
            if at is not None:
                dst = dst.at[at]
            arrival = lr_sem.at[k, origin] if at is not top else lt_sem.at[k]
            pltpu.make_async_remote_copy(
                src_ref=dst, dst_ref=dst, send_sem=ls_sem.at[k, 0], recv_sem=arrival,
                device_id=at_plane(gx), device_id_type=MESH).wait_recv()

        def keep(k):
            return pltpu.make_async_copy(piece(slots + k), place(k, grp), keep_sem.at[k])

        def hold(j):
            return pltpu.make_async_copy(piece(j), pools[0].at[j - fixed], home_sem.at[j - fixed])

        def weight_to(o):
            return pltpu.make_async_remote_copy(
                src_ref=w_ref, dst_ref=wall.at[grp],
                send_sem=ws_sem.at[o], recv_sem=wr_sem.at[grp],
                device_id=at_plane(lax.rem(grp + o, n_grp)), device_id_type=MESH)

        def weight_from(o):
            other = lax.rem(grp + o, n_grp)
            return pltpu.make_async_remote_copy(
                src_ref=w_ref, dst_ref=wall.at[other],
                send_sem=ws_sem.at[o], recv_sem=wr_sem.at[other],
                device_id=at_plane(other), device_id_type=MESH)

        for n in range(3):
            hop(0, n).start()
        for j in range(fixed, slots):
            hold(j).start()
        for k in range(spare):
            keep(k).start()
        for o in range(1, n_grp):
            weight_to(o).start()
        wall[grp] = w_ref[...]

    acc[...] = jnp.zeros(acc.shape, F32)
    ttab[...] = left_terms(time_terms(snaps))
    atab[...] = left_terms(angle_terms(mode_ref[...], angles, 0, angles))
    late = partner(n_sec - 1, me, n_sec)
    late_at = pl.multiple_of(late * q_loc, SUB)
    ltab[...] = left_terms(angle_terms(mode_ref[...], angles, late_at, q_loc))
    total = float(cells * n_grp)

    if spare:
        def fill(j):
            home, found, from_g, from_k = plan(j)
            foreign = jnp.where(home, 0, found)
            first = jnp.where(jnp.logical_and(foreign == 1, from_k == 0), from_g + offset, j - fixed)
            second = jnp.where(jnp.logical_and(foreign == 1, from_k == 1), 1, 0)
            both = spare > 1 and j > fixed

            @pl.loop(0, snaps, unroll=UNROLL)
            def _(t):
                x = pools[0][first, t]
                if both:
                    x = jnp.where(second == 1, pools[1][from_g, t], x)
                stage[j - fixed, t] = x

        for k in range(spare):
            came(k, gx)
            hop(k, 3).start()
            came(k, gy)
            hop(k, 4).start()
            if k + 1 < spare:
                for n in range(3):
                    hop(k + 1, n).start()
            hop(k, 5).start()
            hop(k, 6).start()
            came(k, gxy, bottom)
            came(k, gxy, top)
            hop(k, 7).start()
            for g in (gc, flip(gx, core), flip(gy, core), flip(gxy, core)):
                came(k, g)
            keep(k).wait()
            if k == 0:
                for j in range(fixed, slots):
                    hold(j).wait()
            js = range(fixed, slots) if spare == 1 else (range(fixed, fixed + 1) if k == 0 else range(fixed + 1, slots))
            for j in js:
                fill(j)
                launch([j])
        for o in range(1, n_grp):
            weight_from(o).wait_recv()

    rank = me + side * (n_sec - 1 - 2 * me)

    def holding(sub):
        slot, have = jnp.int32(0), jnp.int32(0)
        for j, (z, s) in enumerate(table):
            if s == sub:
                slot += jnp.where(rank == z, j, 0)
                have += jnp.where(rank == z, 1, 0)
        return slot, have

    def weight_row(sub):
        slot, _ = holding(sub)
        lane = iota((1, LANES), 1)
        row = iota((blocks, LANES), 0)
        if spare:
            home, found, from_g, from_k = plan(slot)
            g = jnp.where(home, grp, from_g)
            b = jnp.where(home, slot, slots + from_k)
            used = jnp.where(home, 1, found)
            live = jnp.int32(0)
            w = jnp.zeros((1, LANES), F32)
            for h in range(n_grp):
                live += jnp.where(g == h, live_ref[h], 0)
                w += jnp.sum(jnp.where(row == jnp.where(g == h, b, -1), wall[h], 0.0), axis=0, keepdims=True)
            live = jnp.where(used == 1, live, 0)
        else:
            b, live = slot, live_ref[grp]
            w = jnp.sum(jnp.where(row == b, w_ref[...], 0.0), axis=0, keepdims=True)
        return jnp.where(b * LANES + lane < live, w / total, 0.0)

    wide = 2

    def to_spectra(j, src):
        for g in range(0, q_loc, wide * SUB):
            x = jnp.concatenate(
                [recv[j, src, :, g + u * SUB:g + (u + 1) * SUB, :].reshape(snaps * SUB, LANES) for u in range(wide)],
                axis=1)
            y = dot(ttab[...], right_terms(x))
            for u in range(wide):
                at = pl.multiple_of(src * q_loc + g + u * SUB, SUB)
                spec[:, pl.ds(at, SUB), :] = y[:, u * LANES:(u + 1) * LANES].reshape(snaps, SUB, LANES)

    stage_rows = acc.shape[1] // STAGES

    def pair(t):
        at = pl.ds(t * stage_rows, stage_rows)
        return pltpu.make_async_remote_copy(
            src_ref=acc.at[pl.ds((1 - side) * near, near), at, :], dst_ref=pbuf.at[:, at, :],
            send_sem=pa_sem.at[t], recv_sem=pr_sem.at[t],
            device_id={"tile": tile + 1 - 2 * side}, device_id_type=MESH)

    def share(o, t, arriving=False):
        other = lax.rem(mine + o, near)
        at = pl.ds(t * stage_rows, stage_rows)
        slot = other if arriving else mine
        return pltpu.make_async_remote_copy(
            src_ref=pacc.at[other, at, :], dst_ref=reda.at[slot, at, :],
            send_sem=sa_sem.at[t, other], recv_sem=ra_sem.at[t, slot],
            device_id={"tile": other // n_role * 2 + side, "role": other % n_role}, device_id_type=MESH)

    def forward(t):
        pair(t).wait_recv()
        at = pl.ds(t * stage_rows, stage_rows)
        pacc[:, at, :] = acc[pl.ds(side * near, near), at, :] + pbuf[:, at, :]
        for o in range(1, near):
            share(o, t).start()

    def arrive(i, j):
        src = partner(i, me, n_sec)
        pltpu.make_async_remote_copy(
            src_ref=recv.at[j, src], dst_ref=recv.at[j, src],
            send_sem=send_sem.at[j], recv_sem=recv_sem.at[j, src],
            device_id={"sec": src}, device_id_type=MESH).wait_recv()
        to_spectra(j, src)

    def to_modal(f, y):
        zbuf[pl.ds(f, modes, stride=snaps), :] = y[:modes, :LANES] + y[modes:, LANES:]
        zbuf[pl.ds(half + f, modes, stride=snaps), :] = y[:modes, LANES:] - y[modes:, :LANES]

    def products(f):
        x = jnp.concatenate([spec[f], spec[half + f]], axis=1)
        return dot(atab[...], right_terms(x))

    def process(j):
        early = j == subs - 1
        pltpu.make_async_copy(piece(0), recv.at[j, me], own_sem.at[j]).wait()
        to_spectra(j, me)

        @pl.loop(1, n_sec - 1 if early else n_sec)
        def _(i):
            arrive(i, j)

        if early:
            spec[:, pl.ds(late_at, q_loc), :] = jnp.zeros((snaps, q_loc, LANES), F32)

            @pl.loop(0, half)
            def _(f):
                ypart[f] = products(f)

            arrive(n_sec - 1, j)

            @pl.loop(0, half, unroll=UNROLL)
            def _(f):
                x = jnp.concatenate([spec[f, pl.ds(late_at, q_loc), :], spec[half + f, pl.ds(late_at, q_loc), :]], axis=1)
                to_modal(f, ypart[f] + dot(ltab[...], right_terms(x)))
        else:
            @pl.loop(0, half)
            def _(f):
                to_modal(f, products(f))

        weight = weight_row(j)
        block = iota((snaps, LANES), 1) // snaps
        steps = SUB // part

        def gram(h):
            rows = []
            for u in range(steps):
                at = pl.multiple_of((h * steps + u) * LANES, LANES)
                z = zbuf[pl.ds(at, LANES), :]
                zh, zl = halves(z)
                g4 = dot(left_terms(z * weight), jnp.concatenate([zh, zl, zh], axis=1), (((1,), (1,)), ((), ())))
                r = g4[:snaps]
                for b in range(1, pack):
                    r = jnp.where(block == b, g4[b * snaps:(b + 1) * snaps], r)
                rows.append(r)
            at = pl.multiple_of(h * SUB, SUB)
            for g in range(n_grp):
                new = jnp.concatenate([r[g * part:(g + 1) * part] for r in rows], axis=0)
                to = g // n_role % 2 * near + g // n_role // 2 * n_role + g % n_role
                acc[to, pl.ds(at, SUB), :] += new

        size = modes // pack // steps // STAGES
        if not early:
            pl.loop(0, size * STAGES)(gram)
            return
        for t in range(STAGES):
            pl.loop(t * size, (t + 1) * size, unroll=UNROLL)(gram)
            pair(t).start()
            if t > 0:
                forward(t - 1)

    for j in range(subs - 1):
        pl.when(holding(j)[1] == 1)(functools.partial(process, j))
    process(subs - 1)

    def last(s, slot):
        return pltpu.make_async_remote_copy(
            src_ref=sb.at[s], dst_ref=redb.at[slot],
            send_sem=sb_sem.at[s], recv_sem=rb_sem.at[slot],
            device_id={"sec": s}, device_id_type=MESH)

    forward(STAGES - 1)
    rows = sb.shape[1]
    for t in range(STAGES):
        for o in range(1, near):
            share(o, t, True).wait_recv()
        for s in range(t * n_sec // STAGES, (t + 1) * n_sec // STAGES):
            value = pacc[mine, s * rows:(s + 1) * rows, :]
            for o in range(1, near):
                value += reda[lax.rem(mine + o, near), s * rows:(s + 1) * rows, :]
            sb[s] = value

            @pl.when(me != s)
            def _():
                last(s, me).start()

    value = sb[me]
    for o in range(1, n_sec):
        s = lax.rem(me + o, n_sec)
        last(s, s).wait_recv()
        value += redb[s]
    out_ref[...] = value

    for j in range(slots):
        @pl.when(owner(j) != me)
        def _():
            outgoing(j).wait_send()
    if spare:
        for k in range(spare):
            for n in range(len(hops)):
                hop(k, n).wait_send()
        for o in range(1, n_grp):
            weight_to(o).wait_send()
    for t in range(STAGES):
        pair(t).wait_send()
        for o in range(1, near):
            share(o, t).wait_send()
    for o in range(1, n_sec):
        last(lax.rem(me + o, n_sec), me).wait_send()


def on_device(pressure, cell_weight, live_cells, mode_order):
    n_sec, n_tile, n_role = (lax.axis_size(a) for a in ("sec", "tile", "role"))
    n_grp = n_tile * n_role
    snaps, q_loc, cells = pressure.shape
    modes = mode_order.shape[0]
    angles = q_loc * n_sec
    blocks = cells // LANES
    subs = blocks // n_sec
    pack = LANES // snaps
    part = snaps // n_grp
    rows = modes // pack * part
    own_rows = rows // n_sec
    vmem = pl.BlockSpec(memory_space=pltpu.VMEM)
    dma = pltpu.SemaphoreType.DMA
    adaptive = subs == 2 and n_grp == blocks and n_role == 2 and n_sec == 4 and q_loc % 16 == 0
    floor = -(-(cells // 3) // LANES)

    def scratch(slots):
        shapes = [
            pltpu.VMEM((subs, n_sec, snaps, q_loc, LANES), F32),
            pltpu.VMEM((snaps, angles, LANES), F32),
            pltpu.VMEM((modes * snaps, LANES), F32),
            pltpu.VMEM((n_grp, rows, LANES), F32),
            pltpu.VMEM((n_grp // 2, rows, LANES), F32),
            pltpu.VMEM((n_grp // 2, rows, LANES), F32),
            pltpu.VMEM((n_grp // 2, rows, LANES), F32),
            pltpu.VMEM((n_sec, own_rows, LANES), F32),
            pltpu.VMEM((n_sec, own_rows, LANES), F32),
            pltpu.VMEM((snaps * SUB, 3 * snaps * SUB), BF16),
            pltpu.VMEM((2 * modes, 3 * angles), BF16),
            pltpu.VMEM((2 * modes, 3 * q_loc), BF16),
            pltpu.VMEM((snaps // 2, 2 * modes, 2 * LANES), F32),
            dma((slots,) if adaptive else (subs, n_sec)), dma((subs, n_sec)), dma((subs,)),
            dma((STAGES,)), dma((STAGES,)), dma((STAGES, n_grp // 2)), dma((STAGES, n_grp // 2)), dma((n_sec,)), dma((n_sec,)),
        ]
        spare = blocks - slots
        if adaptive and spare:
            block = (snaps, q_loc, LANES)
            extra = slots - floor
            shapes += [pltpu.VMEM((n_grp + (extra if k == 0 else 0), *block), F32) for k in range(spare)]
            shapes += [
                pltpu.VMEM((extra, *block), F32),
                pltpu.VMEM((n_grp, blocks, LANES), F32),
                dma((extra,)), dma((spare,)), dma((spare, n_grp)), dma((spare, n_grp)), dma((spare,)), dma((n_grp,)), dma((n_grp,)),
            ]
        return shapes

    def call(slots):
        body = functools.partial(ragged, slots, floor) if adaptive else kernel
        return pl.pallas_call(
            functools.partial(body, n_sec, n_tile, n_role),
            out_shape=jax.ShapeDtypeStruct((own_rows, LANES), F32),
            in_specs=[pl.BlockSpec(memory_space=pl.ANY), vmem, pl.BlockSpec(memory_space=pltpu.SMEM), vmem],
            out_specs=vmem,
            scratch_shapes=scratch(slots),
            compiler_params=pltpu.CompilerParams(
                collective_id=blocks - slots, has_side_effects=True, vmem_limit_bytes=62 * 2**20),
            name="spod",
        )

    args = (pressure, cell_weight.reshape(blocks, LANES), live_cells, mode_order.reshape(1, modes))
    if adaptive:
        count = jnp.maximum((live_cells + (LANES - 1)) // LANES, floor)
        low = blocks - 2
        code = jnp.sum(count + 256 * (count <= floor) + 4096 * (count > low) + 65536 * (count > low + 1))
        total, short = code % 256, code // 256 % 16
        over, more = code // 4096 % 16, code // 65536
        tight = jnp.logical_and(total <= low * n_grp, jnp.logical_or(short <= over, more == 0))
        pick = jnp.where(tight, 2, jnp.where(total <= (low + 1) * n_grp, 1, 0))
        packed = lax.switch(pick, [call(blocks), call(blocks - 1), call(blocks - 2)], *args)
    else:
        packed = call(blocks)(*args)
    out = packed.reshape(modes // pack // n_sec, part, pack, snaps)
    return out.transpose(0, 2, 1, 3).reshape(modes // n_sec, part, snaps)


def solution(mesh):
    in_specs = (P(None, "sec", ("tile", "role")), P(("tile", "role")), P(), P())
    out_specs = P("sec", ("tile", "role"), None)
    return jax.shard_map(
        on_device, mesh=mesh, in_specs=in_specs, out_specs=out_specs, check_vma=False
    )
```

```python
import functools
import math

import jax
import jax.numpy as jnp
from jax import lax
from jax.experimental import pallas as pl
from jax.experimental.pallas import tpu as pltpu
from jax.sharding import PartitionSpec as P

MESH = pl.DeviceIdType.MESH
LANES = 128
UNROLL = 4
STAGES = 4
SUB = 8
VARIANTS = (0, 2, 3, 4, 5)
F32 = jnp.float32
BF16 = jnp.bfloat16


def halves(x):
    hi = x.astype(BF16)
    lo = (x - hi.astype(F32)).astype(BF16)
    return hi, lo


def left_terms(x):
    hi, lo = halves(x)
    return jnp.concatenate([hi, hi, lo], axis=1)


def right_terms(x):
    hi, lo = halves(x)
    return jnp.concatenate([hi, lo, hi], axis=0)


def dot(a, b, dims=(((1,), (0,)), ((), ()))):
    return lax.dot_general(a, b, dims, preferred_element_type=F32)


def partner(x, me, n):
    other, bit = 0, 1
    while bit < n:
        other += (me // bit + x // bit) % 2 * bit
        bit *= 2
    return other


def iota(shape, axis):
    return lax.broadcasted_iota(jnp.int32, shape, axis)


def time_terms(snaps):
    size = snaps * SUB
    row, col = iota((size, size), 0), iota((size, size), 1)
    half = snaps // 2
    r, t = row // SUB, col // SUB
    f = r % half
    hann = 0.5 - 0.5 * jnp.cos((2.0 * math.pi / snaps) * t.astype(F32))
    phase = (2.0 * math.pi / snaps) * ((f * t) % snaps).astype(F32)
    wave = jnp.where(r < half, jnp.cos(phase), -jnp.sin(phase))
    value = math.sqrt(8.0 / (3.0 * snaps)) * hann * wave
    return jnp.where(row % SUB == col % SUB, value, 0.0)


def angle_terms(modes_row, angles, first, count):
    index = first + iota((count, modes_row.shape[1]), 0)
    phase = (2.0 * math.pi / angles) * ((modes_row * index) % angles).astype(F32)
    scale = 1.0 / math.sqrt(angles)
    return jnp.concatenate([(jnp.cos(phase) * scale).T, (jnp.sin(phase) * scale).T], axis=0)


def kernel(n_sec, n_tile, n_role, p_ref, w_ref, live_ref, mode_ref, out_ref,
           recv, spec, zbuf, acc, pbuf, pacc, reda, sb, redb, ttab, atab, ltab, ypart,
           send_sem, recv_sem, own_sem, pa_sem, pr_sem, sa_sem, ra_sem, sb_sem, rb_sem):
    me = lax.axis_index("sec")
    tile, role = lax.axis_index("tile"), lax.axis_index("role")
    n_grp = n_tile * n_role
    grp = tile * n_role + role
    near = n_grp // 2
    side, mine = tile % 2, tile // 2 * n_role + role
    snaps, q_loc, cells = p_ref.shape
    half = snaps // 2
    angles = q_loc * n_sec
    modes = mode_ref.shape[1]
    cell_dev = cells // n_sec
    subs = cell_dev // LANES
    pack = LANES // snaps
    part = snaps // n_grp
    split = q_loc % 16 == 0

    def peer(o):
        other = lax.rem(grp + o, n_grp)
        return other, {"tile": other // n_role, "role": other % n_role}

    barrier = pltpu.get_barrier_semaphore()
    for o in range(1, n_sec):
        pl.semaphore_signal(barrier, inc=1, device_id={"sec": lax.rem(me + o, n_sec)}, device_id_type=MESH)
    for o in range(1, n_grp):
        pl.semaphore_signal(barrier, inc=1, device_id=peer(o)[1], device_id_type=MESH)
    pl.semaphore_wait(barrier, n_sec + n_grp - 2)

    def piece(owner, j):
        start = pl.multiple_of(owner * cell_dev + j * LANES, LANES)
        return p_ref.at[:, :, pl.ds(start, LANES)]

    def outgoing(i, j):
        dest = partner(i, me, n_sec)
        return pltpu.make_async_remote_copy(
            src_ref=piece(dest, j), dst_ref=recv.at[j, me],
            send_sem=send_sem.at[j, dest], recv_sem=recv_sem.at[j, me],
            device_id={"sec": dest}, device_id_type=MESH)

    def own(j):
        return pltpu.make_async_copy(piece(me, j), recv.at[j, me], own_sem.at[j])

    for j in range(subs):
        @pl.loop(1, n_sec)
        def _(i):
            outgoing(i, j).start()
    for j in range(subs):
        own(j).start()

    ttab[...] = left_terms(time_terms(snaps))
    atab[...] = left_terms(angle_terms(mode_ref[...], angles, 0, angles))
    late = partner(n_sec - 1, me, n_sec)
    late_at = pl.multiple_of(late * q_loc, SUB)
    if split:
        ltab[...] = left_terms(angle_terms(mode_ref[...], angles, late_at, q_loc))
    live = live_ref[grp]
    total = float(cells * n_grp)
    wide = 2 if q_loc % (2 * SUB) == 0 else 1

    def to_spectra(j, src):
        for g in range(0, q_loc, wide * SUB):
            x = jnp.concatenate(
                [recv[j, src, :, g + u * SUB:g + (u + 1) * SUB, :].reshape(snaps * SUB, LANES) for u in range(wide)],
                axis=1)
            y = dot(ttab[...], right_terms(x))
            for u in range(wide):
                at = pl.multiple_of(src * q_loc + g + u * SUB, SUB)
                spec[:, pl.ds(at, SUB), :] = y[:, u * LANES:(u + 1) * LANES].reshape(snaps, SUB, LANES)

    stage_rows = acc.shape[1] // STAGES

    def pair(t):
        at = pl.ds(t * stage_rows, stage_rows)
        return pltpu.make_async_remote_copy(
            src_ref=acc.at[pl.ds((1 - side) * near, near), at, :], dst_ref=pbuf.at[:, at, :],
            send_sem=pa_sem.at[t], recv_sem=pr_sem.at[t],
            device_id={"tile": tile + 1 - 2 * side}, device_id_type=MESH)

    def share(o, t, arriving=False):
        other = lax.rem(mine + o, near)
        at = pl.ds(t * stage_rows, stage_rows)
        slot = other if arriving else mine
        return pltpu.make_async_remote_copy(
            src_ref=pacc.at[other, at, :], dst_ref=reda.at[slot, at, :],
            send_sem=sa_sem.at[t, other], recv_sem=ra_sem.at[t, slot],
            device_id={"tile": other // n_role * 2 + side, "role": other % n_role}, device_id_type=MESH)

    def forward(t):
        pair(t).wait_recv()
        at = pl.ds(t * stage_rows, stage_rows)
        pacc[:, at, :] = acc[pl.ds(side * near, near), at, :] + pbuf[:, at, :]
        for o in range(1, near):
            share(o, t).start()

    def arrive(i, j):
        src = partner(i, me, n_sec)
        pltpu.make_async_remote_copy(
            src_ref=recv.at[j, src], dst_ref=recv.at[j, src],
            send_sem=send_sem.at[j, src], recv_sem=recv_sem.at[j, src],
            device_id={"sec": src}, device_id_type=MESH).wait_recv()
        to_spectra(j, src)

    def to_modal(f, y):
        zbuf[pl.ds(f, modes, stride=snaps), :] = y[:modes, :LANES] + y[modes:, LANES:]
        zbuf[pl.ds(half + f, modes, stride=snaps), :] = y[:modes, LANES:] - y[modes:, :LANES]

    def products(f):
        x = jnp.concatenate([spec[f], spec[half + f]], axis=1)
        return dot(atab[...], right_terms(x))

    for j in range(subs):
        own(j).wait()
        to_spectra(j, me)
        early = split and j == subs - 1

        @pl.loop(1, n_sec - 1 if early else n_sec)
        def _(i):
            arrive(i, j)

        if early:
            spec[:, pl.ds(late_at, q_loc), :] = jnp.zeros((snaps, q_loc, LANES), F32)

            @pl.loop(0, half)
            def _(f):
                ypart[f] = products(f)

            arrive(n_sec - 1, j)

            @pl.loop(0, half, unroll=UNROLL)
            def _(f):
                x = jnp.concatenate([spec[f, pl.ds(late_at, q_loc), :], spec[half + f, pl.ds(late_at, q_loc), :]], axis=1)
                to_modal(f, ypart[f] + dot(ltab[...], right_terms(x)))
        else:
            @pl.loop(0, half, unroll=UNROLL)
            def _(f):
                to_modal(f, products(f))

        first = pl.multiple_of(me * cell_dev + j * LANES, LANES)
        position = first + iota((1, LANES), 1)
        weight = jnp.where(position < live, w_ref[pl.ds(me * subs + j, 1), :] / total, 0.0)
        block = iota((snaps, LANES), 1) // snaps
        steps = SUB // part

        def gram(h):
            rows = []
            for u in range(steps):
                at = pl.multiple_of((h * steps + u) * LANES, LANES)
                z = zbuf[pl.ds(at, LANES), :]
                zh, zl = halves(z)
                g4 = dot(left_terms(z * weight), jnp.concatenate([zh, zl, zh], axis=1), (((1,), (1,)), ((), ())))
                r = g4[:snaps]
                for b in range(1, pack):
                    r = jnp.where(block == b, g4[b * snaps:(b + 1) * snaps], r)
                rows.append(r)
            at = pl.multiple_of(h * SUB, SUB)
            for g in range(n_grp):
                new = jnp.concatenate([r[g * part:(g + 1) * part] for r in rows], axis=0)
                to = g // n_role % 2 * near + g // n_role // 2 * n_role + g % n_role
                if j == 0:
                    acc[to, pl.ds(at, SUB), :] = new
                else:
                    acc[to, pl.ds(at, SUB), :] += new

        count = modes // pack // steps // STAGES
        for t in range(STAGES):
            pl.loop(t * count, (t + 1) * count, unroll=UNROLL)(gram)
            if j == subs - 1:
                pair(t).start()
                if t > 0:
                    forward(t - 1)

    def last(s, slot):
        return pltpu.make_async_remote_copy(
            src_ref=sb.at[s], dst_ref=redb.at[slot],
            send_sem=sb_sem.at[s], recv_sem=rb_sem.at[slot],
            device_id={"sec": s}, device_id_type=MESH)

    forward(STAGES - 1)
    rows = sb.shape[1]
    for t in range(STAGES):
        for o in range(1, near):
            share(o, t, True).wait_recv()
        for s in range(t * n_sec // STAGES, (t + 1) * n_sec // STAGES):
            value = pacc[mine, s * rows:(s + 1) * rows, :]
            for o in range(1, near):
                value += reda[lax.rem(mine + o, near), s * rows:(s + 1) * rows, :]
            sb[s] = value

            @pl.when(me != s)
            def _():
                last(s, me).start()

    value = sb[me]
    for o in range(1, n_sec):
        s = lax.rem(me + o, n_sec)
        last(s, s).wait_recv()
        value += redb[s]
    out_ref[...] = value

    for j in range(subs):
        @pl.loop(1, n_sec)
        def _(i):
            outgoing(i, j).wait_send()
    for t in range(STAGES):
        pair(t).wait_send()
        for o in range(1, near):
            share(o, t).wait_send()
    for o in range(1, n_sec):
        last(lax.rem(me + o, n_sec), me).wait_send()


def flip(x, bit):
    return x + bit - 2 * bit * (x // bit % 2)


def slot_table(slots, n_sec, subs):
    half = n_sec // 2
    table = [None] * slots
    for right in (1, 0):
        mine = range(1 - right, slots, 2)
        pad = subs * half - len(mine)
        for i, j in enumerate(mine):
            at = half - 1 - (i + pad) % half
            table[j] = (half + at if right else half - 1 - at, (i + pad) // half)
    return table


def ragged(units, floor, n_sec, n_tile, n_role, *refs):
    n_grp = n_tile * n_role
    near = n_grp // 2
    (p_ref, w_ref, live_ref, mode_ref, out_ref,
     recv, spec, zbuf, acc, pbuf, pacc, reda, sb, redb, ttab, atab, ltab, ypart,
     send_sem, recv_sem, own_sem, pa_sem, pr_sem, sa_sem, ra_sem, sb_sem, rb_sem) = refs[:27]
    extra = refs[27:]
    me = lax.axis_index("sec")
    tile, role = lax.axis_index("tile"), lax.axis_index("role")
    grp = tile * n_role + role
    side, mine = tile % 2, tile // 2 * n_role + role
    snaps, q_loc, cells = p_ref.shape
    half = snaps // 2
    angles = q_loc * n_sec
    modes = mode_ref.shape[1]
    blocks = cells // LANES
    subs = recv.shape[0]
    pack = LANES // snaps
    part = snaps // n_grp
    cut = LANES // 2
    whole, odd = units // 2, units % 2
    slots = whole + odd
    spare = blocks - whole
    fixed = floor if spare else slots
    middle = snaps // 2
    bottom, top = pl.ds(0, middle), pl.ds(middle, middle)
    table = slot_table(slots, n_sec, subs)
    core, xbit, ybit = n_role, 1, 2 * n_role
    if spare:
        pools, stage, wall, home_sem, keep_sem, ls_sem, lr_sem, lt_sem, ws_sem, wr_sem = (
            extra[:spare], *extra[spare:])


    def at_plane(g):
        return {"tile": g // n_role, "role": g % n_role}

    barrier = pltpu.get_barrier_semaphore()
    for o in range(1, n_sec):
        pl.semaphore_signal(barrier, inc=1, device_id={"sec": lax.rem(me + o, n_sec)}, device_id_type=MESH)
    for o in range(1, n_grp):
        pl.semaphore_signal(barrier, inc=1, device_id=at_plane(lax.rem(grp + o, n_grp)), device_id_type=MESH)
    pl.semaphore_wait(barrier, n_sec + n_grp - 2)

    def piece(j):
        return p_ref.at[:, :, pl.ds(j * LANES, LANES)]

    def content(j):
        if j < fixed:
            return piece(j)
        return stage.at[j - fixed] if j < whole else stage.at[j - fixed, bottom]

    def target(j):
        return recv.at[table[j][1], me] if j < whole else recv.at[table[j][1], me, bottom]

    def owner(j):
        z = table[j][0]
        return z + side * (n_sec - 1 - 2 * z)

    def outgoing(j):
        sub = table[j][1]
        return pltpu.make_async_remote_copy(
            src_ref=content(j), dst_ref=target(j),
            send_sem=send_sem.at[j], recv_sem=recv_sem.at[sub, me],
            device_id={"sec": owner(j)}, device_id_type=MESH)

    def own(j):
        sub = table[j][1]
        return pltpu.make_async_copy(content(j), target(j), own_sem.at[sub])

    def is_far(j):
        return owner(j) // (n_sec // 2) != me // (n_sec // 2)

    def launch(js):
        for j in js:
            @pl.when(is_far(j))
            def _():
                outgoing(j).start()
        for j in js:
            @pl.when(jnp.logical_and(jnp.logical_not(is_far(j)), owner(j) != me))
            def _():
                outgoing(j).start()

            @pl.when(owner(j) == me)
            def _():
                own(j).start()

    launch(range(fixed))

    if spare:
        count = [jnp.maximum((live_ref[g] + (cut - 1)) // cut, 2 * fixed) for g in range(n_grp)]
        spaces = [sum(jnp.where(count[g] <= u, 1, 0) for g in range(n_grp)) for u in range(2 * fixed, units)]
        offers, supply = [], jnp.int32(0)
        for u in range(units, 2 * blocks):
            for g in range(n_grp):
                has = count[g] > u
                offers.append((jnp.where(has, supply, -1), n_grp * u + g))
                supply += jnp.where(has, 1, 0)

    def plan(u):
        home_count, want = jnp.int32(0), jnp.int32(0)
        for g in range(n_grp):
            home_count += jnp.where(grp == g, count[g], 0)
            want += jnp.where(jnp.logical_and(g < grp, count[g] <= u), 1, 0)
        for i, space in enumerate(spaces):
            want += jnp.where(2 * fixed + i < u, space, 0)
        code = jnp.int32(0)
        for at, value in offers:
            code += jnp.where(at == want, value, 0)
        home = u < home_count
        used = jnp.where(home, 1, jnp.where(want < supply, 1, 0))
        return jnp.where(home, n_grp * u + grp, code), used, jnp.where(home, 0, used)

    if spare:
        gx, gy, gc = flip(grp, xbit), flip(grp, ybit), flip(grp, core)
        gxy = flip(gx, ybit)
        offset = slots - fixed

        def place(k, g):
            return pools[k].at[g + (offset if k == 0 else 0)]

        hops = [(grp, gx, None), (grp, gy, None), (grp, gc, None), (gx, gy, bottom), (gy, gx, top),
                (gx, gc, None), (gy, gc, None), (gxy, gc, None)]

        def hop(k, n):
            origin, to, at = hops[n]
            src = piece(whole + k) if n < 3 else place(k, origin)
            dst = place(k, origin)
            if at is not None:
                src, dst = src.at[at], dst.at[at]
            arrival = lr_sem.at[k, origin] if at is not top else lt_sem.at[k]
            return pltpu.make_async_remote_copy(
                src_ref=src, dst_ref=dst, send_sem=ls_sem.at[k, n], recv_sem=arrival,
                device_id=at_plane(to), device_id_type=MESH)

        def came(k, origin, at=None):
            dst = place(k, origin)
            if at is not None:
                dst = dst.at[at]
            arrival = lr_sem.at[k, origin] if at is not top else lt_sem.at[k]
            pltpu.make_async_remote_copy(
                src_ref=dst, dst_ref=dst, send_sem=ls_sem.at[k, 0], recv_sem=arrival,
                device_id=at_plane(gx), device_id_type=MESH).wait_recv()

        def keep(k):
            return pltpu.make_async_copy(piece(whole + k), place(k, grp), keep_sem.at[k])

        def hold(j):
            return pltpu.make_async_copy(piece(j), pools[0].at[j - fixed], home_sem.at[j - fixed])

        def weight_to(o):
            return pltpu.make_async_remote_copy(
                src_ref=w_ref, dst_ref=wall.at[grp],
                send_sem=ws_sem.at[o], recv_sem=wr_sem.at[grp],
                device_id=at_plane(lax.rem(grp + o, n_grp)), device_id_type=MESH)

        def weight_from(o):
            other = lax.rem(grp + o, n_grp)
            return pltpu.make_async_remote_copy(
                src_ref=w_ref, dst_ref=wall.at[other],
                send_sem=ws_sem.at[o], recv_sem=wr_sem.at[other],
                device_id=at_plane(other), device_id_type=MESH)

        for n in range(3):
            hop(0, n).start()
        for j in range(fixed, slots):
            hold(j).start()
        for k in range(spare):
            keep(k).start()
        for o in range(1, n_grp):
            weight_to(o).start()
        wall[grp] = w_ref[...]

    acc[...] = jnp.zeros(acc.shape, F32)
    ttab[...] = left_terms(time_terms(snaps))
    atab[...] = left_terms(angle_terms(mode_ref[...], angles, 0, angles))
    late = partner(n_sec - 1, me, n_sec)
    late_at = pl.multiple_of(late * q_loc, SUB)
    ltab[...] = left_terms(angle_terms(mode_ref[...], angles, late_at, q_loc))
    total = float(cells * n_grp)

    if spare:
        low = iota((1, 1, LANES), 2) < cut

        def source(u, depth):
            code, _, foreign = plan(u)
            unit, g = code // n_grp, code % n_grp
            from_k = unit // 2 - whole
            first = jnp.where(jnp.logical_and(foreign == 1, from_k == 0), g + offset, u // 2 - fixed)
            flipped = unit % 2

            def read(t, high):
                x = pools[0][first, pl.ds(t, 1)]
                for k in range(1, depth + 1):
                    x = jnp.where(jnp.logical_and(foreign == 1, from_k == k), pools[k][g, pl.ds(t, 1)], x)
                return jnp.where(flipped == high, x, pltpu.roll(x, cut, 2))
            return read

        def fill(j, depth):
            left = source(2 * j, depth)
            if j < whole:
                right = source(2 * j + 1, depth)

                @pl.loop(0, snaps)
                def _(t):
                    stage[j - fixed, pl.ds(t, 1)] = jnp.where(low, left(t, 0), right(t, 1))
            else:
                @pl.loop(0, middle)
                def _(t):
                    stage[j - fixed, pl.ds(t, 1)] = jnp.where(low, left(t, 0), left(t + middle, 1))

        for k in range(spare):
            came(k, gx)
            hop(k, 3).start()
            came(k, gy)
            hop(k, 4).start()
            if k + 1 < spare:
                for n in range(3):
                    hop(k + 1, n).start()
            hop(k, 5).start()
            hop(k, 6).start()
            came(k, gxy, bottom)
            came(k, gxy, top)
            hop(k, 7).start()
            for g in (gc, flip(gx, core), flip(gy, core), flip(gxy, core)):
                came(k, g)
            keep(k).wait()
            if k == 0:
                for j in range(fixed, slots):
                    hold(j).wait()
            for j in range(fixed, slots):
                if min(j - fixed, spare - 1) == k:
                    fill(j, k)
                    launch([j])
        for o in range(1, n_grp):
            weight_from(o).wait_recv()

    rank = me + side * (n_sec - 1 - 2 * me)

    def holding(sub):
        slot, have = jnp.int32(0), jnp.int32(0)
        for j, (z, at) in enumerate(table):
            hit = jnp.logical_and(rank == z, sub == at)
            slot += jnp.where(hit, j, 0)
            have += jnp.where(hit, 1, 0)
        return slot, have

    def weight_row(slot):
        lane = iota((1, LANES), 1)
        row = iota((blocks, LANES), 0)
        if not spare:
            w = jnp.sum(jnp.where(row == slot, w_ref[...], 0.0), axis=0, keepdims=True)
            return jnp.where(slot * LANES + lane < live_ref[grp], w / total, 0.0)

        def unit_row(high):
            code, used, _ = plan(2 * slot + high)
            unit, g = code // n_grp, code % n_grp
            live = jnp.int32(0)
            w = jnp.zeros((1, LANES), F32)
            for h in range(n_grp):
                live += jnp.where(g == h, live_ref[h], 0)
                w += jnp.sum(jnp.where(row == jnp.where(g == h, unit // 2, -1), wall[h], 0.0), axis=0, keepdims=True)
            w = jnp.where(unit % 2 == high, w, jnp.concatenate([w[:, cut:], w[:, :cut]], axis=1))
            if high and odd:
                used = jnp.where(slot < whole, used, 0)
            return jnp.where(unit * cut + lane % cut < jnp.where(used == 1, live, 0), w / total, 0.0)
        return jnp.where(lane < cut, unit_row(0), unit_row(1))

    wide = 2

    def to_spectra(j, src):
        @pl.loop(0, q_loc // (wide * SUB), unroll=2)
        def _(i):
            g = pl.multiple_of(i * (wide * SUB), wide * SUB)
            x = jnp.concatenate(
                [recv[j, src, :, pl.ds(g + u * SUB, SUB), :].reshape(snaps * SUB, LANES) for u in range(wide)],
                axis=1)
            y = dot(ttab[...], right_terms(x))
            for u in range(wide):
                at = pl.multiple_of(src * q_loc + g + u * SUB, SUB)
                spec[:, pl.ds(at, SUB), :] = y[:, u * LANES:(u + 1) * LANES].reshape(snaps, SUB, LANES)

    stage_rows = acc.shape[1] // STAGES

    def pair(t):
        at = pl.ds(t * stage_rows, stage_rows)
        return pltpu.make_async_remote_copy(
            src_ref=acc.at[pl.ds((1 - side) * near, near), at, :], dst_ref=pbuf.at[:, at, :],
            send_sem=pa_sem.at[t], recv_sem=pr_sem.at[t],
            device_id={"tile": tile + 1 - 2 * side}, device_id_type=MESH)

    def share(o, t, arriving=False):
        other = lax.rem(mine + o, near)
        at = pl.ds(t * stage_rows, stage_rows)
        slot = other if arriving else mine
        return pltpu.make_async_remote_copy(
            src_ref=pacc.at[other, at, :], dst_ref=reda.at[slot, at, :],
            send_sem=sa_sem.at[t, other], recv_sem=ra_sem.at[t, slot],
            device_id={"tile": other // n_role * 2 + side, "role": other % n_role}, device_id_type=MESH)

    def forward(t):
        pair(t).wait_recv()
        at = pl.ds(t * stage_rows, stage_rows)
        pacc[:, at, :] = acc[pl.ds(side * near, near), at, :] + pbuf[:, at, :]
        for o in range(1, near):
            share(o, t).start()

    def unpack(j, src):
        @pl.loop(0, middle)
        def _(t):
            recv[j, src, pl.ds(t + middle, 1)] = pltpu.roll(recv[j, src, pl.ds(t, 1)], cut, 2)

    def landed(j, src, short):
        def wait(dst):
            pltpu.make_async_remote_copy(
                src_ref=dst, dst_ref=dst, send_sem=send_sem.at[0], recv_sem=recv_sem.at[j, src],
                device_id={"sec": src}, device_id_type=MESH).wait_recv()

        if not odd:
            wait(recv.at[j, src])
            return

        @pl.when(short)
        def _():
            wait(recv.at[j, src, bottom])
            unpack(j, src)

        @pl.when(jnp.logical_not(short))
        def _():
            wait(recv.at[j, src])

    def landed_own(j, short):
        def wait(dst):
            pltpu.make_async_copy(dst, dst, own_sem.at[j]).wait()

        if not odd:
            wait(recv.at[j, me])
            return

        @pl.when(short)
        def _():
            wait(recv.at[j, me, bottom])
            unpack(j, me)

        @pl.when(jnp.logical_not(short))
        def _():
            wait(recv.at[j, me])

    def arrive(i, j, short):
        src = partner(i, me, n_sec)
        landed(j, src, short)
        to_spectra(j, src)

    def to_modal(f, y):
        zbuf[pl.ds(f, modes, stride=snaps), :] = y[:modes, :LANES] + y[modes:, LANES:]
        zbuf[pl.ds(half + f, modes, stride=snaps), :] = y[:modes, LANES:] - y[modes:, :LANES]

    def products(f):
        x = jnp.concatenate([spec[f], spec[half + f]], axis=1)
        return dot(atab[...], right_terms(x))

    def process(j, slot):
        short = slot >= whole
        landed_own(j, short)
        to_spectra(j, me)

        @pl.loop(1, n_sec - 1)
        def _(i):
            arrive(i, j, short)

        spec[:, pl.ds(late_at, q_loc), :] = jnp.zeros((snaps, q_loc, LANES), F32)

        @pl.loop(0, half)
        def _(f):
            ypart[f] = products(f)

        weight = weight_row(slot)
        arrive(n_sec - 1, j, short)

        @pl.loop(0, half, unroll=UNROLL)
        def _(f):
            x = jnp.concatenate([spec[f, pl.ds(late_at, q_loc), :], spec[half + f, pl.ds(late_at, q_loc), :]], axis=1)
            to_modal(f, ypart[f] + dot(ltab[...], right_terms(x)))

        block = iota((snaps, LANES), 1) // snaps
        steps = SUB // part

        def gram(h):
            rows = []
            for u in range(steps):
                at = pl.multiple_of((h * steps + u) * LANES, LANES)
                z = zbuf[pl.ds(at, LANES), :]
                zh, zl = halves(z)
                g4 = dot(left_terms(z * weight), jnp.concatenate([zh, zl, zh], axis=1), (((1,), (1,)), ((), ())))
                r = g4[:snaps]
                for b in range(1, pack):
                    r = jnp.where(block == b, g4[b * snaps:(b + 1) * snaps], r)
                rows.append(r)
            at = pl.multiple_of(h * SUB, SUB)
            for g in range(n_grp):
                new = jnp.concatenate([r[g * part:(g + 1) * part] for r in rows], axis=0)
                to = g // n_role % 2 * near + g // n_role // 2 * n_role + g % n_role
                acc[to, pl.ds(at, SUB), :] += new

        size = modes // pack // steps // STAGES
        for t in range(STAGES):
            pl.loop(t * size, (t + 1) * size, unroll=UNROLL)(gram)

            @pl.when(j == subs - 1)
            def _():
                pair(t).start()
                if t > 0:
                    forward(t - 1)

    @pl.loop(0, subs)
    def _(j):
        slot, have = holding(j)
        pl.when(have == 1)(functools.partial(process, j, slot))

    def last(s, slot):
        return pltpu.make_async_remote_copy(
            src_ref=sb.at[s], dst_ref=redb.at[slot],
            send_sem=sb_sem.at[s], recv_sem=rb_sem.at[slot],
            device_id={"sec": s}, device_id_type=MESH)

    forward(STAGES - 1)
    rows = sb.shape[1]
    for t in range(STAGES):
        for o in range(1, near):
            share(o, t, True).wait_recv()
        for s in range(t * n_sec // STAGES, (t + 1) * n_sec // STAGES):
            value = pacc[mine, s * rows:(s + 1) * rows, :]
            for o in range(1, near):
                value += reda[lax.rem(mine + o, near), s * rows:(s + 1) * rows, :]
            sb[s] = value

            @pl.when(me != s)
            def _():
                last(s, me).start()

    value = sb[me]
    for o in range(1, n_sec):
        s = lax.rem(me + o, n_sec)
        last(s, s).wait_recv()
        value += redb[s]
    out_ref[...] = value

    for j in range(slots):
        @pl.when(owner(j) != me)
        def _():
            outgoing(j).wait_send()
    if spare:
        for k in range(spare):
            for n in range(len(hops)):
                hop(k, n).wait_send()
        for o in range(1, n_grp):
            weight_to(o).wait_send()
    for t in range(STAGES):
        pair(t).wait_send()
        for o in range(1, near):
            share(o, t).wait_send()
    for o in range(1, n_sec):
        last(lax.rem(me + o, n_sec), me).wait_send()


def choose(blocks, floor, live_ref, out_ref):
    cut, top = LANES // 2, 2 * blocks
    n_grp = live_ref.shape[0]
    count = [jnp.maximum((live_ref[g] + (cut - 1)) // cut, 2 * floor) for g in range(n_grp)]
    above = {u: sum(jnp.where(c > u, 1, 0) for c in count) for u in range(2 * floor, top)}

    def fits(units):
        whole = units // 2
        spare = blocks - whole
        stages = [sum(above[u] for u in range(max(units, 2 * (whole + k)), 2 * (whole + k) + 2)) for k in range(spare)]
        supply = sum(stages)
        good = supply <= sum(n_grp - above[u] for u in range(2 * floor, units))
        for k in range(spare - 1):
            space = sum(n_grp - above[u] for u in range(2 * floor, 2 * (floor + k) + 2))
            good = jnp.logical_and(good, jnp.minimum(space, supply) <= sum(stages[:k + 1]))
        return good

    pick = jnp.int32(0)
    for number, less in enumerate(VARIANTS):
        if number:
            pick = jnp.where(fits(top - less), number, pick)
    out_ref[0] = pick


def on_device(pressure, cell_weight, live_cells, mode_order):
    n_sec, n_tile, n_role = (lax.axis_size(a) for a in ("sec", "tile", "role"))
    n_grp = n_tile * n_role
    snaps, q_loc, cells = pressure.shape
    modes = mode_order.shape[0]
    angles = q_loc * n_sec
    blocks = cells // LANES
    subs = blocks // n_sec
    pack = LANES // snaps
    part = snaps // n_grp
    rows = modes // pack * part
    own_rows = rows // n_sec
    vmem = pl.BlockSpec(memory_space=pltpu.VMEM)
    dma = pltpu.SemaphoreType.DMA
    adaptive = subs == 2 and n_grp == blocks and n_role == 2 and n_sec == 4 and q_loc % 16 == 0
    floor = -(-(cells // 3) // LANES)

    def scratch(units):
        whole = units // 2
        slots = whole + units % 2
        shapes = [
            pltpu.VMEM((subs, n_sec, snaps, q_loc, LANES), F32),
            pltpu.VMEM((snaps, angles, LANES), F32),
            pltpu.VMEM((modes * snaps, LANES), F32),
            pltpu.VMEM((n_grp, rows, LANES), F32),
            pltpu.VMEM((n_grp // 2, rows, LANES), F32),
            pltpu.VMEM((n_grp // 2, rows, LANES), F32),
            pltpu.VMEM((n_grp // 2, rows, LANES), F32),
            pltpu.VMEM((n_sec, own_rows, LANES), F32),
            pltpu.VMEM((n_sec, own_rows, LANES), F32),
            pltpu.VMEM((snaps * SUB, 3 * snaps * SUB), BF16),
            pltpu.VMEM((2 * modes, 3 * angles), BF16),
            pltpu.VMEM((2 * modes, 3 * q_loc), BF16),
            pltpu.VMEM((snaps // 2, 2 * modes, 2 * LANES), F32),
            dma((slots,) if adaptive else (subs, n_sec)), dma((subs, n_sec)), dma((subs,)),
            dma((STAGES,)), dma((STAGES,)), dma((STAGES, n_grp // 2)), dma((STAGES, n_grp // 2)), dma((n_sec,)), dma((n_sec,)),
        ]
        spare = blocks - whole
        if adaptive and spare:
            block = (snaps, q_loc, LANES)
            extra = slots - floor
            shapes += [pltpu.VMEM((n_grp + (extra if k == 0 else 0), *block), F32) for k in range(spare)]
            shapes += [
                pltpu.VMEM((extra, *block), F32),
                pltpu.VMEM((n_grp, blocks, LANES), F32),
                dma((extra,)), dma((spare,)), dma((spare, SUB)), dma((spare, n_grp)), dma((spare,)), dma((n_grp,)), dma((n_grp,)),
            ]
        return shapes

    def call(units, number=0):
        body = functools.partial(ragged, units, floor) if adaptive else kernel
        return pl.pallas_call(
            functools.partial(body, n_sec, n_tile, n_role),
            out_shape=jax.ShapeDtypeStruct((own_rows, LANES), F32),
            in_specs=[pl.BlockSpec(memory_space=pl.ANY), vmem, pl.BlockSpec(memory_space=pltpu.SMEM), vmem],
            out_specs=vmem,
            scratch_shapes=scratch(units),
            compiler_params=pltpu.CompilerParams(
                collective_id=number, has_side_effects=True, vmem_limit_bytes=62 * 2**20),
            name="spod",
        )

    args = (pressure, cell_weight.reshape(blocks, LANES), live_cells, mode_order.reshape(1, modes))
    if adaptive:
        top = 2 * blocks
        pick = pl.pallas_call(
            functools.partial(choose, blocks, floor),
            out_shape=jax.ShapeDtypeStruct((1,), jnp.int32),
            in_specs=[pl.BlockSpec(memory_space=pltpu.SMEM)],
            out_specs=pl.BlockSpec(memory_space=pltpu.SMEM),
            name="choose",
        )(live_cells)[0]
        packed = lax.switch(pick, [call(top - less, number) for number, less in enumerate(VARIANTS)], *args)
    else:
        packed = call(2 * blocks)(*args)
    out = packed.reshape(modes // pack // n_sec, part, pack, snaps)
    return out.transpose(0, 2, 1, 3).reshape(modes // n_sec, part, snaps)


def solution(mesh):
    in_specs = (P(None, "sec", ("tile", "role")), P(("tile", "role")), P(), P())
    out_specs = P("sec", ("tile", "role"), None)
    return jax.shard_map(
        on_device, mesh=mesh, in_specs=in_specs, out_specs=out_specs, check_vma=False
    )
```

```python
import functools
import math

import jax
import jax.numpy as jnp
from jax import lax
from jax.experimental import pallas as pl
from jax.experimental.pallas import tpu as pltpu
from jax.sharding import PartitionSpec as P

MESH = pl.DeviceIdType.MESH
LANES = 128
UNROLL = 4
STAGES = 4
SUB = 8
QUAD = 4
VARIANTS = (0, 4, 6, 8, 10)
F32 = jnp.float32
BF16 = jnp.bfloat16


def halves(x):
    hi = x.astype(BF16)
    lo = (x - hi.astype(F32)).astype(BF16)
    return hi, lo


def left_terms(x):
    hi, lo = halves(x)
    return jnp.concatenate([hi, hi, lo], axis=1)


def right_terms(x):
    hi, lo = halves(x)
    return jnp.concatenate([hi, lo, hi], axis=0)


def dot(a, b, dims=(((1,), (0,)), ((), ()))):
    return lax.dot_general(a, b, dims, preferred_element_type=F32)


def partner(x, me, n):
    other, bit = 0, 1
    while bit < n:
        other += (me // bit + x // bit) % 2 * bit
        bit *= 2
    return other


def iota(shape, axis):
    return lax.broadcasted_iota(jnp.int32, shape, axis)


def time_terms(snaps, first=0, count=None):
    size = snaps * SUB
    shape = (size if count is None else count, size)
    row, col = first + iota(shape, 0), iota(shape, 1)
    half = snaps // 2
    r, t = row // SUB, col // SUB
    f = r % half
    hann = 0.5 - 0.5 * jnp.cos((2.0 * math.pi / snaps) * t.astype(F32))
    phase = (2.0 * math.pi / snaps) * ((f * t) % snaps).astype(F32)
    wave = jnp.where(r < half, jnp.cos(phase), -jnp.sin(phase))
    value = math.sqrt(8.0 / (3.0 * snaps)) * hann * wave
    return jnp.where(row % SUB == col % SUB, value, 0.0)


def angle_terms(modes_row, angles, first, count):
    index = first + iota((count, modes_row.shape[1]), 0)
    phase = (2.0 * math.pi / angles) * ((modes_row * index) % angles).astype(F32)
    scale = 1.0 / math.sqrt(angles)
    return jnp.concatenate([(jnp.cos(phase) * scale).T, (jnp.sin(phase) * scale).T], axis=0)


def kernel(n_sec, n_tile, n_role, p_ref, w_ref, live_ref, mode_ref, out_ref,
           recv, spec, zbuf, acc, pbuf, pacc, reda, sb, redb, ttab, atab, ltab, ypart,
           send_sem, recv_sem, own_sem, pa_sem, pr_sem, sa_sem, ra_sem, sb_sem, rb_sem):
    me = lax.axis_index("sec")
    tile, role = lax.axis_index("tile"), lax.axis_index("role")
    n_grp = n_tile * n_role
    grp = tile * n_role + role
    near = n_grp // 2
    side, mine = tile % 2, tile // 2 * n_role + role
    snaps, q_loc, cells = p_ref.shape
    half = snaps // 2
    angles = q_loc * n_sec
    modes = mode_ref.shape[1]
    cell_dev = cells // n_sec
    subs = cell_dev // LANES
    pack = LANES // snaps
    part = snaps // n_grp
    split = q_loc % 16 == 0

    def peer(o):
        other = lax.rem(grp + o, n_grp)
        return other, {"tile": other // n_role, "role": other % n_role}

    barrier = pltpu.get_barrier_semaphore()
    for o in range(1, n_sec):
        pl.semaphore_signal(barrier, inc=1, device_id={"sec": lax.rem(me + o, n_sec)}, device_id_type=MESH)
    for o in range(1, n_grp):
        pl.semaphore_signal(barrier, inc=1, device_id=peer(o)[1], device_id_type=MESH)
    pl.semaphore_wait(barrier, n_sec + n_grp - 2)

    def piece(owner, j):
        start = pl.multiple_of(owner * cell_dev + j * LANES, LANES)
        return p_ref.at[:, :, pl.ds(start, LANES)]

    def outgoing(i, j):
        dest = partner(i, me, n_sec)
        return pltpu.make_async_remote_copy(
            src_ref=piece(dest, j), dst_ref=recv.at[j, me],
            send_sem=send_sem.at[j, dest], recv_sem=recv_sem.at[j, me],
            device_id={"sec": dest}, device_id_type=MESH)

    def own(j):
        return pltpu.make_async_copy(piece(me, j), recv.at[j, me], own_sem.at[j])

    for j in range(subs):
        @pl.loop(1, n_sec)
        def _(i):
            outgoing(i, j).start()
    for j in range(subs):
        own(j).start()

    ttab[...] = left_terms(time_terms(snaps))
    atab[...] = left_terms(angle_terms(mode_ref[...], angles, 0, angles))
    late = partner(n_sec - 1, me, n_sec)
    late_at = pl.multiple_of(late * q_loc, SUB)
    if split:
        ltab[...] = left_terms(angle_terms(mode_ref[...], angles, late_at, q_loc))
    live = live_ref[grp]
    total = float(cells * n_grp)
    wide = 2 if q_loc % (2 * SUB) == 0 else 1

    def to_spectra(j, src):
        for g in range(0, q_loc, wide * SUB):
            x = jnp.concatenate(
                [recv[j, src, :, g + u * SUB:g + (u + 1) * SUB, :].reshape(snaps * SUB, LANES) for u in range(wide)],
                axis=1)
            y = dot(ttab[...], right_terms(x))
            for u in range(wide):
                at = pl.multiple_of(src * q_loc + g + u * SUB, SUB)
                spec[:, pl.ds(at, SUB), :] = y[:, u * LANES:(u + 1) * LANES].reshape(snaps, SUB, LANES)

    stage_rows = acc.shape[1] // STAGES

    def pair(t):
        at = pl.ds(t * stage_rows, stage_rows)
        return pltpu.make_async_remote_copy(
            src_ref=acc.at[pl.ds((1 - side) * near, near), at, :], dst_ref=pbuf.at[:, at, :],
            send_sem=pa_sem.at[t], recv_sem=pr_sem.at[t],
            device_id={"tile": tile + 1 - 2 * side}, device_id_type=MESH)

    def share(o, t, arriving=False):
        other = lax.rem(mine + o, near)
        at = pl.ds(t * stage_rows, stage_rows)
        slot = other if arriving else mine
        return pltpu.make_async_remote_copy(
            src_ref=pacc.at[other, at, :], dst_ref=reda.at[slot, at, :],
            send_sem=sa_sem.at[t, other], recv_sem=ra_sem.at[t, slot],
            device_id={"tile": other // n_role * 2 + side, "role": other % n_role}, device_id_type=MESH)

    def forward(t):
        pair(t).wait_recv()
        at = pl.ds(t * stage_rows, stage_rows)
        pacc[:, at, :] = acc[pl.ds(side * near, near), at, :] + pbuf[:, at, :]
        for o in range(1, near):
            share(o, t).start()

    def arrive(i, j):
        src = partner(i, me, n_sec)
        pltpu.make_async_remote_copy(
            src_ref=recv.at[j, src], dst_ref=recv.at[j, src],
            send_sem=send_sem.at[j, src], recv_sem=recv_sem.at[j, src],
            device_id={"sec": src}, device_id_type=MESH).wait_recv()
        to_spectra(j, src)

    def to_modal(f, y):
        zbuf[pl.ds(f, modes, stride=snaps), :] = y[:modes, :LANES] + y[modes:, LANES:]
        zbuf[pl.ds(half + f, modes, stride=snaps), :] = y[:modes, LANES:] - y[modes:, :LANES]

    def products(f):
        x = jnp.concatenate([spec[f], spec[half + f]], axis=1)
        return dot(atab[...], right_terms(x))

    for j in range(subs):
        own(j).wait()
        to_spectra(j, me)
        early = split and j == subs - 1

        @pl.loop(1, n_sec - 1 if early else n_sec)
        def _(i):
            arrive(i, j)

        if early:
            spec[:, pl.ds(late_at, q_loc), :] = jnp.zeros((snaps, q_loc, LANES), F32)

            @pl.loop(0, half)
            def _(f):
                ypart[f] = products(f)

            arrive(n_sec - 1, j)

            @pl.loop(0, half, unroll=UNROLL)
            def _(f):
                x = jnp.concatenate([spec[f, pl.ds(late_at, q_loc), :], spec[half + f, pl.ds(late_at, q_loc), :]], axis=1)
                to_modal(f, ypart[f] + dot(ltab[...], right_terms(x)))
        else:
            @pl.loop(0, half, unroll=UNROLL)
            def _(f):
                to_modal(f, products(f))

        first = pl.multiple_of(me * cell_dev + j * LANES, LANES)
        position = first + iota((1, LANES), 1)
        weight = jnp.where(position < live, w_ref[pl.ds(me * subs + j, 1), :] / total, 0.0)
        block = iota((snaps, LANES), 1) // snaps
        steps = SUB // part

        def gram(h):
            rows = []
            for u in range(steps):
                at = pl.multiple_of((h * steps + u) * LANES, LANES)
                z = zbuf[pl.ds(at, LANES), :]
                zh, zl = halves(z)
                g4 = dot(left_terms(z * weight), jnp.concatenate([zh, zl, zh], axis=1), (((1,), (1,)), ((), ())))
                r = g4[:snaps]
                for b in range(1, pack):
                    r = jnp.where(block == b, g4[b * snaps:(b + 1) * snaps], r)
                rows.append(r)
            at = pl.multiple_of(h * SUB, SUB)
            for g in range(n_grp):
                new = jnp.concatenate([r[g * part:(g + 1) * part] for r in rows], axis=0)
                to = g // n_role % 2 * near + g // n_role // 2 * n_role + g % n_role
                if j == 0:
                    acc[to, pl.ds(at, SUB), :] = new
                else:
                    acc[to, pl.ds(at, SUB), :] += new

        count = modes // pack // steps // STAGES
        for t in range(STAGES):
            pl.loop(t * count, (t + 1) * count, unroll=UNROLL)(gram)
            if j == subs - 1:
                pair(t).start()
                if t > 0:
                    forward(t - 1)

    def last(s, slot):
        return pltpu.make_async_remote_copy(
            src_ref=sb.at[s], dst_ref=redb.at[slot],
            send_sem=sb_sem.at[s], recv_sem=rb_sem.at[slot],
            device_id={"sec": s}, device_id_type=MESH)

    forward(STAGES - 1)
    rows = sb.shape[1]
    for t in range(STAGES):
        for o in range(1, near):
            share(o, t, True).wait_recv()
        for s in range(t * n_sec // STAGES, (t + 1) * n_sec // STAGES):
            value = pacc[mine, s * rows:(s + 1) * rows, :]
            for o in range(1, near):
                value += reda[lax.rem(mine + o, near), s * rows:(s + 1) * rows, :]
            sb[s] = value

            @pl.when(me != s)
            def _():
                last(s, me).start()

    value = sb[me]
    for o in range(1, n_sec):
        s = lax.rem(me + o, n_sec)
        last(s, s).wait_recv()
        value += redb[s]
    out_ref[...] = value

    for j in range(subs):
        @pl.loop(1, n_sec)
        def _(i):
            outgoing(i, j).wait_send()
    for t in range(STAGES):
        pair(t).wait_send()
        for o in range(1, near):
            share(o, t).wait_send()
    for o in range(1, n_sec):
        last(lax.rem(me + o, n_sec), me).wait_send()


def flip(x, bit):
    return x + bit - 2 * bit * (x // bit % 2)


def slot_table(slots, n_sec, subs):
    half = n_sec // 2
    table = [None] * slots
    for right in (1, 0):
        mine = range(1 - right, slots, 2)
        pad = subs * half - len(mine)
        for i, j in enumerate(mine):
            at = half - 1 - (i + pad) % half
            table[j] = (half + at if right else half - 1 - at, (i + pad) // half)
    return table


def ragged(units, floor, n_sec, n_tile, n_role, *refs):
    n_grp = n_tile * n_role
    near = n_grp // 2
    (p_ref, w_ref, live_ref, mode_ref, out_ref,
     recv, spec, zbuf, acc, pbuf, pacc, reda, sb, redb, ttab, atab, ltab, ypart,
     send_sem, recv_sem, own_sem, pa_sem, pr_sem, sa_sem, ra_sem, sb_sem, rb_sem) = refs[:27]
    extra = refs[27:]
    me = lax.axis_index("sec")
    tile, role = lax.axis_index("tile"), lax.axis_index("role")
    grp = tile * n_role + role
    side, mine = tile % 2, tile // 2 * n_role + role
    snaps, q_loc, cells = p_ref.shape
    half = snaps // 2
    angles = q_loc * n_sec
    modes = mode_ref.shape[1]
    blocks = cells // LANES
    subs = recv.shape[0]
    pack = LANES // snaps
    part = snaps // n_grp
    cut = LANES // QUAD
    rows_t = snaps // QUAD
    whole, odd = units // QUAD, units % QUAD
    slots = whole + min(odd, 1)
    spare = blocks - whole
    fixed = floor if spare else slots
    middle = snaps // 2
    bottom, top = pl.ds(0, middle), pl.ds(middle, middle)
    short_rows = pl.ds(0, odd * rows_t)
    quarter = iota((1, 1, LANES), 2) // cut
    table = slot_table(slots, n_sec, subs)
    core, xbit, ybit = n_role, 1, 2 * n_role
    if spare:
        pools, stage, wall, home_sem, keep_sem, ls_sem, lr_sem, lt_sem, ws_sem, wr_sem = (
            extra[:spare], *extra[spare:])


    def at_plane(g):
        return {"tile": g // n_role, "role": g % n_role}

    barrier = pltpu.get_barrier_semaphore()
    for o in range(1, n_sec):
        pl.semaphore_signal(barrier, inc=1, device_id={"sec": lax.rem(me + o, n_sec)}, device_id_type=MESH)
    for o in range(1, n_grp):
        pl.semaphore_signal(barrier, inc=1, device_id=at_plane(lax.rem(grp + o, n_grp)), device_id_type=MESH)
    pl.semaphore_wait(barrier, n_sec + n_grp - 2)

    def piece(j):
        return p_ref.at[:, :, pl.ds(j * LANES, LANES)]

    def content(j):
        if j < fixed:
            return piece(j)
        return stage.at[j - fixed] if j < whole else stage.at[j - fixed, short_rows]

    def target(j):
        return recv.at[table[j][1], me] if j < whole else recv.at[table[j][1], me, short_rows]

    def owner(j):
        z = table[j][0]
        return z + side * (n_sec - 1 - 2 * z)

    def outgoing(j):
        sub = table[j][1]
        return pltpu.make_async_remote_copy(
            src_ref=content(j), dst_ref=target(j),
            send_sem=send_sem.at[j], recv_sem=recv_sem.at[sub, me],
            device_id={"sec": owner(j)}, device_id_type=MESH)

    def own(j):
        sub = table[j][1]
        return pltpu.make_async_copy(content(j), target(j), own_sem.at[sub])

    def is_far(j):
        return owner(j) // (n_sec // 2) != me // (n_sec // 2)

    def launch(js):
        for j in js:
            @pl.when(is_far(j))
            def _():
                outgoing(j).start()
        for j in js:
            @pl.when(jnp.logical_and(jnp.logical_not(is_far(j)), owner(j) != me))
            def _():
                outgoing(j).start()

            @pl.when(owner(j) == me)
            def _():
                own(j).start()

    launch(range(fixed))

    if spare:
        least, most = QUAD * fixed, QUAD * blocks
        count = [jnp.maximum((live_ref[g] + (cut - 1)) // cut, least) for g in range(n_grp)]
        shape = (-(-(most - units) // SUB) * SUB, LANES)
        unit_of, grp_of = units + iota(shape, 0), iota(shape, 1)
        place_of, given = jnp.zeros(shape, jnp.int32), jnp.zeros(shape, jnp.int32)
        supply = jnp.int32(0)
        for g in range(n_grp):
            more = jnp.where(count[g] > unit_of, 1, 0)
            given += jnp.where(grp_of == g, more, 0)
            place_of += jnp.maximum(jnp.minimum(unit_of, count[g]) - units, 0) + jnp.where(grp_of > g, more, 0)
            supply += jnp.maximum(count[g] - units, 0)
        key_of = jnp.where(given == 1, place_of, -1)

    def plan(u):
        home_count, want = jnp.int32(0), jnp.int32(0)
        for g in range(n_grp):
            home_count += jnp.where(grp == g, count[g], 0)
            want += jnp.maximum(u - count[g], 0) + jnp.where(jnp.logical_and(g < grp, count[g] <= u), 1, 0)
        code = jnp.sum(jnp.where(key_of == want, n_grp * unit_of + grp_of, 0))
        home = u < home_count
        used = jnp.where(home, 1, jnp.where(want < supply, 1, 0))
        return jnp.where(home, n_grp * u + grp, code), used, jnp.where(home, 0, used)

    def turn(x, amount, axis):
        x = jnp.where(amount % 2 == 1, pltpu.roll(x, cut, axis), x)
        return jnp.where(amount // 2 == 1, pltpu.roll(x, 2 * cut, axis), x)

    if spare:
        gx, gy, gc = flip(grp, xbit), flip(grp, ybit), flip(grp, core)
        gxy = flip(gx, ybit)
        offset = slots - fixed

        def place(k, g):
            return pools[k].at[g + (offset if k == 0 else 0)]

        hops = [(grp, gx, bottom), (grp, gy, top), (grp, gx, top), (grp, gy, bottom), (grp, gc, None),
                (gx, gy, bottom), (gy, gx, top), (gx, gc, None), (gy, gc, None), (gxy, gc, None)]

        def hop(k, n):
            origin, to, at = hops[n]
            src = piece(whole + k) if n < 5 else place(k, origin)
            dst = place(k, origin)
            if at is not None:
                src, dst = src.at[at], dst.at[at]
            arrival = lr_sem.at[k, origin] if at is not top else lt_sem.at[k, origin]
            return pltpu.make_async_remote_copy(
                src_ref=src, dst_ref=dst, send_sem=ls_sem.at[k, n], recv_sem=arrival,
                device_id=at_plane(to), device_id_type=MESH)

        def came(k, origin, at=None):
            dst = place(k, origin)
            if at is not None:
                dst = dst.at[at]
            arrival = lr_sem.at[k, origin] if at is not top else lt_sem.at[k, origin]
            pltpu.make_async_remote_copy(
                src_ref=dst, dst_ref=dst, send_sem=ls_sem.at[k, 0], recv_sem=arrival,
                device_id=at_plane(gx), device_id_type=MESH).wait_recv()

        def keep(k):
            return pltpu.make_async_copy(piece(whole + k), place(k, grp), keep_sem.at[k])

        def hold(j):
            return pltpu.make_async_copy(piece(j), pools[0].at[j - fixed], home_sem.at[j - fixed])

        def weight_to(o):
            return pltpu.make_async_remote_copy(
                src_ref=w_ref, dst_ref=wall.at[grp],
                send_sem=ws_sem.at[o], recv_sem=wr_sem.at[grp],
                device_id=at_plane(lax.rem(grp + o, n_grp)), device_id_type=MESH)

        def weight_from(o):
            other = lax.rem(grp + o, n_grp)
            return pltpu.make_async_remote_copy(
                src_ref=w_ref, dst_ref=wall.at[other],
                send_sem=ws_sem.at[o], recv_sem=wr_sem.at[other],
                device_id=at_plane(other), device_id_type=MESH)

        for n in range(5):
            hop(0, n).start()
        for j in range(fixed, slots):
            hold(j).start()
        for k in range(spare):
            keep(k).start()
        for o in range(1, n_grp):
            weight_to(o).start()
        wall[grp] = w_ref[...]

    acc[...] = jnp.zeros(acc.shape, F32)

    @pl.loop(0, snaps * SUB // 16)
    def _(i):
        at = pl.multiple_of(i * 16, 16)
        ttab[pl.ds(at, 16), :] = left_terms(time_terms(snaps, at, 16))

    @pl.loop(0, angles // LANES)
    def _(i):
        at = pl.multiple_of(i * LANES, LANES)
        hi, lo = halves(angle_terms(mode_ref[...], angles, at, LANES))
        for n, x in enumerate((hi, hi, lo)):
            atab[:, pl.ds(n * angles + at, LANES)] = x

    late = partner(n_sec - 1, me, n_sec)
    late_at = pl.multiple_of(late * q_loc, SUB)
    ltab[...] = left_terms(angle_terms(mode_ref[...], angles, late_at, q_loc))
    total = float(cells * n_grp)

    if spare:
        def source(u, depth):
            code, _, foreign = plan(u)
            unit, g = code // n_grp, code % n_grp
            from_k = unit // QUAD - whole
            first = jnp.where(jnp.logical_and(foreign == 1, from_k == 0), g + offset, u // QUAD - fixed)

            def read(t, to):
                x = pools[0][first, pl.ds(t, 1)]
                for k in range(1, depth + 1):
                    x = jnp.where(jnp.logical_and(foreign == 1, from_k == k), pools[k][g, pl.ds(t, 1)], x)
                return turn(x, (to + QUAD - unit % QUAD) % QUAD, 2)
            return read

        def fill(j, depth):
            if j < whole:
                reads = [source(QUAD * j + i, depth) for i in range(QUAD)]

                @pl.loop(0, snaps)
                def _(t):
                    x = reads[0](t, 0)
                    for i in range(1, QUAD):
                        x = jnp.where(quarter == i, reads[i](t, i), x)
                    stage[j - fixed, pl.ds(t, 1)] = x
                return
            for i in range(odd):
                read = source(QUAD * j + i, depth)

                @pl.loop(0, rows_t)
                def _(r):
                    x = read(r, 0)
                    for b in range(1, QUAD):
                        x = jnp.where(quarter == b, read(b * rows_t + r, b), x)
                    stage[j - fixed, pl.ds(i * rows_t + r, 1)] = x

        def advance(k):
            came(k, gx, bottom)
            hop(k, 5).start()
            came(k, gy, top)
            hop(k, 6).start()
            if k + 1 < spare:
                for n in range(5):
                    hop(k + 1, n).start()
            came(k, gx, top)
            hop(k, 7).start()
            came(k, gy, bottom)
            hop(k, 8).start()
            came(k, gxy, bottom)
            came(k, gxy, top)
            hop(k, 9).start()
            for g in (gc, flip(gx, core), flip(gy, core), flip(gxy, core)):
                came(k, g)
            keep(k).wait()
            if k == 0:
                for j in range(fixed, slots):
                    hold(j).wait()
            for j in range(fixed, slots):
                if min(j - fixed, spare - 1) == k:
                    fill(j, k)
                    launch([j])

        for k in range(min(spare, 2)):
            advance(k)
        for o in range(1, n_grp):
            weight_from(o).wait_recv()

    rank = me + side * (n_sec - 1 - 2 * me)

    def holding(sub):
        slot, have = jnp.int32(0), jnp.int32(0)
        for j, (z, at) in enumerate(table):
            hit = jnp.logical_and(rank == z, sub == at)
            slot += jnp.where(hit, j, 0)
            have += jnp.where(hit, 1, 0)
        return slot, have

    def weight_row(slot):
        lane = iota((1, LANES), 1)
        row = iota((blocks, LANES), 0)
        if not spare:
            w = jnp.sum(jnp.where(row == slot, w_ref[...], 0.0), axis=0, keepdims=True)
            return jnp.where(slot * LANES + lane < live_ref[grp], w / total, 0.0)

        def unit_row(i):
            code, used, _ = plan(QUAD * slot + i)
            unit, g = code // n_grp, code % n_grp
            live = jnp.int32(0)
            w = jnp.zeros((blocks, LANES), F32)
            for h in range(n_grp):
                live += jnp.where(g == h, live_ref[h], 0)
                w += jnp.where(row == jnp.where(g == h, unit // QUAD, -1), wall[h], 0.0)
            w = jnp.sum(turn(w, (i + QUAD - unit % QUAD) % QUAD, 1), axis=0, keepdims=True)
            if odd and i >= odd:
                used = jnp.where(slot < whole, used, 0)
            return jnp.where(unit * cut + lane % cut < jnp.where(used == 1, live, 0), w / total, 0.0)

        w = unit_row(0)
        for i in range(1, QUAD):
            w = jnp.where(lane // cut == i, unit_row(i), w)
        return w

    wide = 2

    def to_spectra(j, src):
        @pl.loop(0, q_loc // (wide * SUB), unroll=2)
        def _(i):
            g = pl.multiple_of(i * (wide * SUB), wide * SUB)
            x = jnp.concatenate(
                [recv[j, src, :, pl.ds(g + u * SUB, SUB), :].reshape(snaps * SUB, LANES) for u in range(wide)],
                axis=1)
            y = dot(ttab[...], right_terms(x))
            for u in range(wide):
                at = pl.multiple_of(src * q_loc + g + u * SUB, SUB)
                spec[:, pl.ds(at, SUB), :] = y[:, u * LANES:(u + 1) * LANES].reshape(snaps, SUB, LANES)

    stage_rows = acc.shape[1] // STAGES

    def pair(t):
        at = pl.ds(pl.multiple_of(t * stage_rows, SUB), stage_rows)
        return pltpu.make_async_remote_copy(
            src_ref=acc.at[pl.ds((1 - side) * near, near), at, :], dst_ref=pbuf.at[:, at, :],
            send_sem=pa_sem.at[t], recv_sem=pr_sem.at[t],
            device_id={"tile": tile + 1 - 2 * side}, device_id_type=MESH)

    def share(o, t, arriving=False):
        other = lax.rem(mine + o, near)
        at = pl.ds(pl.multiple_of(t * stage_rows, SUB), stage_rows)
        slot = other if arriving else mine
        return pltpu.make_async_remote_copy(
            src_ref=pacc.at[other, at, :], dst_ref=reda.at[slot, at, :],
            send_sem=sa_sem.at[t, other], recv_sem=ra_sem.at[t, slot],
            device_id={"tile": other // n_role * 2 + side, "role": other % n_role}, device_id_type=MESH)

    def forward(t):
        pair(t).wait_recv()
        at = pl.ds(pl.multiple_of(t * stage_rows, SUB), stage_rows)
        pacc[:, at, :] = acc[pl.ds(side * near, near), at, :] + pbuf[:, at, :]
        for o in range(1, near):
            share(o, t).start()

    def unpack(j, src):
        @pl.loop(0, rows_t)
        def _(r):
            packed = [recv[j, src, pl.ds(i * rows_t + r, 1)] for i in range(odd)]
            for b in range(QUAD):
                x = pltpu.roll(packed[0], (QUAD - b) % QUAD * cut, 2) if b else packed[0]
                for i in range(1, odd):
                    move = (i + QUAD - b) % QUAD * cut
                    x = jnp.where(quarter == i, pltpu.roll(packed[i], move, 2) if move else packed[i], x)
                recv[j, src, pl.ds(b * rows_t + r, 1)] = x

    def landed(j, src, short):
        def wait(dst):
            pltpu.make_async_remote_copy(
                src_ref=dst, dst_ref=dst, send_sem=send_sem.at[0], recv_sem=recv_sem.at[j, src],
                device_id={"sec": src}, device_id_type=MESH).wait_recv()

        if not odd:
            wait(recv.at[j, src])
            return

        @pl.when(short)
        def _():
            wait(recv.at[j, src, short_rows])
            unpack(j, src)

        @pl.when(jnp.logical_not(short))
        def _():
            wait(recv.at[j, src])

    def landed_own(j, short):
        def wait(dst):
            pltpu.make_async_copy(dst, dst, own_sem.at[j]).wait()

        if not odd:
            wait(recv.at[j, me])
            return

        @pl.when(short)
        def _():
            wait(recv.at[j, me, short_rows])
            unpack(j, me)

        @pl.when(jnp.logical_not(short))
        def _():
            wait(recv.at[j, me])

    def arrive(i, j, short):
        src = partner(i, me, n_sec)
        landed(j, src, short)
        to_spectra(j, src)

    def to_modal(f, y):
        zbuf[pl.ds(f, modes, stride=snaps), :] = y[:modes, :LANES] + y[modes:, LANES:]
        zbuf[pl.ds(half + f, modes, stride=snaps), :] = y[:modes, LANES:] - y[modes:, :LANES]

    def products(f):
        x = jnp.concatenate([spec[f], spec[half + f]], axis=1)
        return dot(atab[...], right_terms(x))

    def process(j, slot):
        short = slot >= whole
        landed_own(j, short)
        to_spectra(j, me)

        @pl.loop(1, n_sec - 1)
        def _(i):
            arrive(i, j, short)

        spec[:, pl.ds(late_at, q_loc), :] = jnp.zeros((snaps, q_loc, LANES), F32)

        @pl.loop(0, half)
        def _(f):
            ypart[f] = products(f)

        weight = weight_row(slot)
        arrive(n_sec - 1, j, short)

        @pl.loop(0, half, unroll=UNROLL)
        def _(f):
            x = jnp.concatenate([spec[f, pl.ds(late_at, q_loc), :], spec[half + f, pl.ds(late_at, q_loc), :]], axis=1)
            to_modal(f, ypart[f] + dot(ltab[...], right_terms(x)))

        block = iota((snaps, LANES), 1) // snaps
        steps = SUB // part

        def gram(h):
            rows = []
            for u in range(steps):
                at = pl.multiple_of((h * steps + u) * LANES, LANES)
                z = zbuf[pl.ds(at, LANES), :]
                zh, zl = halves(z)
                g4 = dot(left_terms(z * weight), jnp.concatenate([zh, zl, zh], axis=1), (((1,), (1,)), ((), ())))
                r = g4[:snaps]
                for b in range(1, pack):
                    r = jnp.where(block == b, g4[b * snaps:(b + 1) * snaps], r)
                rows.append(r)
            at = pl.multiple_of(h * SUB, SUB)
            for g in range(n_grp):
                new = jnp.concatenate([r[g * part:(g + 1) * part] for r in rows], axis=0)
                to = g // n_role % 2 * near + g // n_role // 2 * n_role + g % n_role
                acc[to, pl.ds(at, SUB), :] += new

        size = modes // pack // steps // STAGES

        @pl.loop(0, STAGES)
        def _(t):
            pl.loop(0, size, unroll=UNROLL)(lambda h: gram(t * size + h))

            @pl.when(j == subs - 1)
            def _():
                pair(t).start()

            @pl.when(jnp.logical_and(j == subs - 1, t > 0))
            def _():
                forward(t - 1)

    @pl.loop(0, subs)
    def _(j):
        slot, have = holding(j)
        pl.when(have == 1)(functools.partial(process, j, slot))
        if spare > 2:
            pl.when(j == 0)(functools.partial(advance, 2))

    def last(s, slot):
        return pltpu.make_async_remote_copy(
            src_ref=sb.at[s], dst_ref=redb.at[slot],
            send_sem=sb_sem.at[s], recv_sem=rb_sem.at[slot],
            device_id={"sec": s}, device_id_type=MESH)

    forward(STAGES - 1)
    rows = sb.shape[1]
    for t in range(STAGES):
        for o in range(1, near):
            share(o, t, True).wait_recv()
        for s in range(t * n_sec // STAGES, (t + 1) * n_sec // STAGES):
            value = pacc[mine, s * rows:(s + 1) * rows, :]
            for o in range(1, near):
                value += reda[lax.rem(mine + o, near), s * rows:(s + 1) * rows, :]
            sb[s] = value

            @pl.when(me != s)
            def _():
                last(s, me).start()

    value = sb[me]
    for o in range(1, n_sec):
        s = lax.rem(me + o, n_sec)
        last(s, s).wait_recv()
        value += redb[s]
    out_ref[...] = value

    for j in range(slots):
        @pl.when(owner(j) != me)
        def _():
            outgoing(j).wait_send()
    if spare:
        for k in range(spare):
            for n in range(len(hops)):
                hop(k, n).wait_send()
        for o in range(1, n_grp):
            weight_to(o).wait_send()
    for t in range(STAGES):
        pair(t).wait_send()
        for o in range(1, near):
            share(o, t).wait_send()
    for o in range(1, n_sec):
        last(lax.rem(me + o, n_sec), me).wait_send()


def choose(blocks, floor, live_ref, out_ref):
    cut, top, least = LANES // QUAD, QUAD * blocks, QUAD * floor
    n_grp = live_ref.shape[0]
    count = [jnp.maximum((live_ref[g] + (cut - 1)) // cut, least) for g in range(n_grp)]
    above = {u: sum(jnp.where(c > u, 1, 0) for c in count) for u in range(least, top)}

    def fits(units):
        whole = units // QUAD
        spare = blocks - whole
        stages = [sum(above[u] for u in range(max(units, QUAD * (whole + k)), QUAD * (whole + k + 1))) for k in range(spare)]
        supply = sum(stages)
        good = supply <= sum(n_grp - above[u] for u in range(least, units))
        for k in range(spare - 1):
            space = sum(n_grp - above[u] for u in range(least, least + QUAD * (k + 1)))
            good = jnp.logical_and(good, jnp.minimum(space, supply) <= sum(stages[:k + 1]))
        return good

    pick = jnp.int32(0)
    for number, less in enumerate(VARIANTS):
        if number:
            pick = jnp.where(fits(top - less), number, pick)
    out_ref[0] = pick


def on_device(pressure, cell_weight, live_cells, mode_order):
    n_sec, n_tile, n_role = (lax.axis_size(a) for a in ("sec", "tile", "role"))
    n_grp = n_tile * n_role
    snaps, q_loc, cells = pressure.shape
    modes = mode_order.shape[0]
    angles = q_loc * n_sec
    blocks = cells // LANES
    subs = blocks // n_sec
    pack = LANES // snaps
    part = snaps // n_grp
    rows = modes // pack * part
    own_rows = rows // n_sec
    vmem = pl.BlockSpec(memory_space=pltpu.VMEM)
    dma = pltpu.SemaphoreType.DMA
    adaptive = subs == 2 and n_grp == blocks and n_role == 2 and n_sec == 4 and q_loc % 16 == 0
    floor = -(-(cells // 3) // LANES)

    def scratch(units):
        whole = units // QUAD
        slots = whole + min(units % QUAD, 1)
        shapes = [
            pltpu.VMEM((subs, n_sec, snaps, q_loc, LANES), F32),
            pltpu.VMEM((snaps, angles, LANES), F32),
            pltpu.VMEM((modes * snaps, LANES), F32),
            pltpu.VMEM((n_grp, rows, LANES), F32),
            pltpu.VMEM((n_grp // 2, rows, LANES), F32),
            pltpu.VMEM((n_grp // 2, rows, LANES), F32),
            pltpu.VMEM((n_grp // 2, rows, LANES), F32),
            pltpu.VMEM((n_sec, own_rows, LANES), F32),
            pltpu.VMEM((n_sec, own_rows, LANES), F32),
            pltpu.VMEM((snaps * SUB, 3 * snaps * SUB), BF16),
            pltpu.VMEM((2 * modes, 3 * angles), BF16),
            pltpu.VMEM((2 * modes, 3 * q_loc), BF16),
            pltpu.VMEM((snaps // 2, 2 * modes, 2 * LANES), F32),
            dma((slots,) if adaptive else (subs, n_sec)), dma((subs, n_sec)), dma((subs,)),
            dma((STAGES,)), dma((STAGES,)), dma((STAGES, n_grp // 2)), dma((STAGES, n_grp // 2)), dma((n_sec,)), dma((n_sec,)),
        ]
        spare = blocks - whole
        if adaptive and spare:
            block = (snaps, q_loc, LANES)
            extra = slots - floor
            shapes += [pltpu.VMEM((n_grp + (extra if k == 0 else 0), *block), F32) for k in range(spare)]
            shapes += [
                pltpu.VMEM((extra, *block), F32),
                pltpu.VMEM((n_grp, blocks, LANES), F32),
                dma((extra,)), dma((spare,)), dma((spare, 10)), dma((spare, n_grp)), dma((spare, n_grp)), dma((n_grp,)), dma((n_grp,)),
            ]
        return shapes

    def call(units, number=0):
        body = functools.partial(ragged, units, floor) if adaptive else kernel
        return pl.pallas_call(
            functools.partial(body, n_sec, n_tile, n_role),
            out_shape=jax.ShapeDtypeStruct((own_rows, LANES), F32),
            in_specs=[pl.BlockSpec(memory_space=pl.ANY), vmem, pl.BlockSpec(memory_space=pltpu.SMEM), vmem],
            out_specs=vmem,
            scratch_shapes=scratch(units),
            compiler_params=pltpu.CompilerParams(
                collective_id=number, has_side_effects=True, vmem_limit_bytes=62 * 2**20),
            name="spod",
        )

    args = (pressure, cell_weight.reshape(blocks, LANES), live_cells, mode_order.reshape(1, modes))
    if adaptive:
        top = QUAD * blocks
        pick = pl.pallas_call(
            functools.partial(choose, blocks, floor),
            out_shape=jax.ShapeDtypeStruct((1,), jnp.int32),
            in_specs=[pl.BlockSpec(memory_space=pltpu.SMEM)],
            out_specs=pl.BlockSpec(memory_space=pltpu.SMEM),
            name="choose",
        )(live_cells)[0]
        packed = lax.switch(pick, [call(top - less, number) for number, less in enumerate(VARIANTS)], *args)
    else:
        packed = call(QUAD * blocks)(*args)
    out = packed.reshape(modes // pack // n_sec, part, pack, snaps)
    return out.transpose(0, 2, 1, 3).reshape(modes // n_sec, part, snaps)


def solution(mesh):
    in_specs = (P(None, "sec", ("tile", "role")), P(("tile", "role")), P(), P())
    out_specs = P("sec", ("tile", "role"), None)
    return jax.shard_map(
        on_device, mesh=mesh, in_specs=in_specs, out_specs=out_specs, check_vma=False
    )
```

```python
import functools
import math

import jax
import jax.numpy as jnp
from jax import lax
from jax.experimental import pallas as pl
from jax.experimental.pallas import tpu as pltpu
from jax.sharding import PartitionSpec as P

MESH = pl.DeviceIdType.MESH
LANES = 128
UNROLL = 4
STAGES = 4
SUB = 8
QUAD = 4
VARIANTS = (0, 4, 6, 8, 10)
F32 = jnp.float32
BF16 = jnp.bfloat16


def halves(x):
    hi = x.astype(BF16)
    lo = (x - hi.astype(F32)).astype(BF16)
    return hi, lo


def left_terms(x):
    hi, lo = halves(x)
    return jnp.concatenate([hi, hi, lo], axis=1)


def right_terms(x):
    hi, lo = halves(x)
    return jnp.concatenate([hi, lo, hi], axis=0)


def dot(a, b, dims=(((1,), (0,)), ((), ()))):
    return lax.dot_general(a, b, dims, preferred_element_type=F32)


def partner(x, me, n):
    other, bit = 0, 1
    while bit < n:
        other += (me // bit + x // bit) % 2 * bit
        bit *= 2
    return other


def iota(shape, axis):
    return lax.broadcasted_iota(jnp.int32, shape, axis)


def time_terms(snaps, first=0, count=None):
    size = snaps * SUB
    shape = (size if count is None else count, size)
    row, col = first + iota(shape, 0), iota(shape, 1)
    half = snaps // 2
    r, t = row // SUB, col // SUB
    f = r % half
    hann = 0.5 - 0.5 * jnp.cos((2.0 * math.pi / snaps) * t.astype(F32))
    phase = (2.0 * math.pi / snaps) * ((f * t) % snaps).astype(F32)
    wave = jnp.where(r < half, jnp.cos(phase), -jnp.sin(phase))
    value = math.sqrt(8.0 / (3.0 * snaps)) * hann * wave
    return jnp.where(row % SUB == col % SUB, value, 0.0)


def angle_terms(modes_row, angles, first, count):
    index = first + iota((count, modes_row.shape[1]), 0)
    phase = (2.0 * math.pi / angles) * ((modes_row * index) % angles).astype(F32)
    scale = 1.0 / math.sqrt(angles)
    return jnp.concatenate([(jnp.cos(phase) * scale).T, (jnp.sin(phase) * scale).T], axis=0)


def kernel(n_sec, n_tile, n_role, p_ref, w_ref, live_ref, mode_ref, out_ref,
           recv, spec, zbuf, acc, pbuf, pacc, reda, sb, redb, ttab, atab, ltab, ypart,
           send_sem, recv_sem, own_sem, pa_sem, pr_sem, sa_sem, ra_sem, sb_sem, rb_sem):
    me = lax.axis_index("sec")
    tile, role = lax.axis_index("tile"), lax.axis_index("role")
    n_grp = n_tile * n_role
    grp = tile * n_role + role
    near = n_grp // 2
    side, mine = tile % 2, tile // 2 * n_role + role
    snaps, q_loc, cells = p_ref.shape
    half = snaps // 2
    angles = q_loc * n_sec
    modes = mode_ref.shape[1]
    cell_dev = cells // n_sec
    subs = cell_dev // LANES
    pack = LANES // snaps
    part = snaps // n_grp
    split = q_loc % 16 == 0

    def peer(o):
        other = lax.rem(grp + o, n_grp)
        return other, {"tile": other // n_role, "role": other % n_role}

    barrier = pltpu.get_barrier_semaphore()
    for o in range(1, n_sec):
        pl.semaphore_signal(barrier, inc=1, device_id={"sec": lax.rem(me + o, n_sec)}, device_id_type=MESH)
    for o in range(1, n_grp):
        pl.semaphore_signal(barrier, inc=1, device_id=peer(o)[1], device_id_type=MESH)
    pl.semaphore_wait(barrier, n_sec + n_grp - 2)

    def piece(owner, j):
        start = pl.multiple_of(owner * cell_dev + j * LANES, LANES)
        return p_ref.at[:, :, pl.ds(start, LANES)]

    def outgoing(i, j):
        dest = partner(i, me, n_sec)
        return pltpu.make_async_remote_copy(
            src_ref=piece(dest, j), dst_ref=recv.at[j, me],
            send_sem=send_sem.at[j, dest], recv_sem=recv_sem.at[j, me],
            device_id={"sec": dest}, device_id_type=MESH)

    def own(j):
        return pltpu.make_async_copy(piece(me, j), recv.at[j, me], own_sem.at[j])

    for j in range(subs):
        @pl.loop(1, n_sec)
        def _(i):
            outgoing(i, j).start()
    for j in range(subs):
        own(j).start()

    ttab[...] = left_terms(time_terms(snaps))
    atab[...] = left_terms(angle_terms(mode_ref[...], angles, 0, angles))
    late = partner(n_sec - 1, me, n_sec)
    late_at = pl.multiple_of(late * q_loc, SUB)
    if split:
        ltab[...] = left_terms(angle_terms(mode_ref[...], angles, late_at, q_loc))
    live = live_ref[grp]
    total = float(cells * n_grp)
    wide = 2 if q_loc % (2 * SUB) == 0 else 1

    def to_spectra(j, src):
        for g in range(0, q_loc, wide * SUB):
            x = jnp.concatenate(
                [recv[j, src, :, g + u * SUB:g + (u + 1) * SUB, :].reshape(snaps * SUB, LANES) for u in range(wide)],
                axis=1)
            y = dot(ttab[...], right_terms(x))
            for u in range(wide):
                at = pl.multiple_of(src * q_loc + g + u * SUB, SUB)
                spec[:, pl.ds(at, SUB), :] = y[:, u * LANES:(u + 1) * LANES].reshape(snaps, SUB, LANES)

    stage_rows = acc.shape[1] // STAGES

    def pair(t):
        at = pl.ds(t * stage_rows, stage_rows)
        return pltpu.make_async_remote_copy(
            src_ref=acc.at[pl.ds((1 - side) * near, near), at, :], dst_ref=pbuf.at[:, at, :],
            send_sem=pa_sem.at[t], recv_sem=pr_sem.at[t],
            device_id={"tile": tile + 1 - 2 * side}, device_id_type=MESH)

    def share(o, t, arriving=False):
        other = lax.rem(mine + o, near)
        at = pl.ds(t * stage_rows, stage_rows)
        slot = other if arriving else mine
        return pltpu.make_async_remote_copy(
            src_ref=pacc.at[other, at, :], dst_ref=reda.at[slot, at, :],
            send_sem=sa_sem.at[t, other], recv_sem=ra_sem.at[t, slot],
            device_id={"tile": other // n_role * 2 + side, "role": other % n_role}, device_id_type=MESH)

    def forward(t):
        pair(t).wait_recv()
        at = pl.ds(t * stage_rows, stage_rows)
        pacc[:, at, :] = acc[pl.ds(side * near, near), at, :] + pbuf[:, at, :]
        for o in range(1, near):
            share(o, t).start()

    def arrive(i, j):
        src = partner(i, me, n_sec)
        pltpu.make_async_remote_copy(
            src_ref=recv.at[j, src], dst_ref=recv.at[j, src],
            send_sem=send_sem.at[j, src], recv_sem=recv_sem.at[j, src],
            device_id={"sec": src}, device_id_type=MESH).wait_recv()
        to_spectra(j, src)

    def to_modal(f, y):
        zbuf[pl.ds(f, modes, stride=snaps), :] = y[:modes, :LANES] + y[modes:, LANES:]
        zbuf[pl.ds(half + f, modes, stride=snaps), :] = y[:modes, LANES:] - y[modes:, :LANES]

    def products(f):
        x = jnp.concatenate([spec[f], spec[half + f]], axis=1)
        return dot(atab[...], right_terms(x))

    for j in range(subs):
        own(j).wait()
        to_spectra(j, me)
        early = split and j == subs - 1

        @pl.loop(1, n_sec - 1 if early else n_sec)
        def _(i):
            arrive(i, j)

        if early:
            spec[:, pl.ds(late_at, q_loc), :] = jnp.zeros((snaps, q_loc, LANES), F32)

            @pl.loop(0, half)
            def _(f):
                ypart[f] = products(f)

            arrive(n_sec - 1, j)

            @pl.loop(0, half, unroll=UNROLL)
            def _(f):
                x = jnp.concatenate([spec[f, pl.ds(late_at, q_loc), :], spec[half + f, pl.ds(late_at, q_loc), :]], axis=1)
                to_modal(f, ypart[f] + dot(ltab[...], right_terms(x)))
        else:
            @pl.loop(0, half, unroll=UNROLL)
            def _(f):
                to_modal(f, products(f))

        first = pl.multiple_of(me * cell_dev + j * LANES, LANES)
        position = first + iota((1, LANES), 1)
        weight = jnp.where(position < live, w_ref[pl.ds(me * subs + j, 1), :] / total, 0.0)
        block = iota((snaps, LANES), 1) // snaps
        steps = SUB // part

        def gram(h):
            rows = []
            for u in range(steps):
                at = pl.multiple_of((h * steps + u) * LANES, LANES)
                z = zbuf[pl.ds(at, LANES), :]
                zh, zl = halves(z)
                g4 = dot(left_terms(z * weight), jnp.concatenate([zh, zl, zh], axis=1), (((1,), (1,)), ((), ())))
                r = g4[:snaps]
                for b in range(1, pack):
                    r = jnp.where(block == b, g4[b * snaps:(b + 1) * snaps], r)
                rows.append(r)
            at = pl.multiple_of(h * SUB, SUB)
            for g in range(n_grp):
                new = jnp.concatenate([r[g * part:(g + 1) * part] for r in rows], axis=0)
                to = g // n_role % 2 * near + g // n_role // 2 * n_role + g % n_role
                if j == 0:
                    acc[to, pl.ds(at, SUB), :] = new
                else:
                    acc[to, pl.ds(at, SUB), :] += new

        count = modes // pack // steps // STAGES
        for t in range(STAGES):
            pl.loop(t * count, (t + 1) * count, unroll=UNROLL)(gram)
            if j == subs - 1:
                pair(t).start()
                if t > 0:
                    forward(t - 1)

    def last(s, slot):
        return pltpu.make_async_remote_copy(
            src_ref=sb.at[s], dst_ref=redb.at[slot],
            send_sem=sb_sem.at[s], recv_sem=rb_sem.at[slot],
            device_id={"sec": s}, device_id_type=MESH)

    forward(STAGES - 1)
    rows = sb.shape[1]
    for t in range(STAGES):
        for o in range(1, near):
            share(o, t, True).wait_recv()
        for s in range(t * n_sec // STAGES, (t + 1) * n_sec // STAGES):
            value = pacc[mine, s * rows:(s + 1) * rows, :]
            for o in range(1, near):
                value += reda[lax.rem(mine + o, near), s * rows:(s + 1) * rows, :]
            sb[s] = value

            @pl.when(me != s)
            def _():
                last(s, me).start()

    value = sb[me]
    for o in range(1, n_sec):
        s = lax.rem(me + o, n_sec)
        last(s, s).wait_recv()
        value += redb[s]
    out_ref[...] = value

    for j in range(subs):
        @pl.loop(1, n_sec)
        def _(i):
            outgoing(i, j).wait_send()
    for t in range(STAGES):
        pair(t).wait_send()
        for o in range(1, near):
            share(o, t).wait_send()
    for o in range(1, n_sec):
        last(lax.rem(me + o, n_sec), me).wait_send()


def stage_blocks(units, blocks):
    return list(range(units // QUAD, blocks))


def flip(x, bit):
    return x + bit - 2 * bit * (x // bit % 2)


def slot_table(slots, n_sec, subs):
    half = n_sec // 2
    table = [None] * slots
    for right in (1, 0):
        mine = range(1 - right, slots, 2)
        pad = subs * half - len(mine)
        for i, j in enumerate(mine):
            at = half - 1 - (i + pad) % half
            table[j] = (half + at if right else half - 1 - at, (i + pad) // half)
    return table


def ragged(units, floor, n_sec, n_tile, n_role, *refs):
    n_grp = n_tile * n_role
    near = n_grp // 2
    (p_ref, w_ref, live_ref, mode_ref, out_ref,
     recv, spec, zbuf, acc, pbuf, pacc, reda, sb, redb, ttab, atab, ltab, ypart,
     send_sem, recv_sem, own_sem, pa_sem, pr_sem, sa_sem, ra_sem, sb_sem, rb_sem) = refs[:27]
    extra = refs[27:]
    me = lax.axis_index("sec")
    tile, role = lax.axis_index("tile"), lax.axis_index("role")
    grp = tile * n_role + role
    side, mine = tile % 2, tile // 2 * n_role + role
    snaps, q_loc, cells = p_ref.shape
    half = snaps // 2
    angles = q_loc * n_sec
    modes = mode_ref.shape[1]
    blocks = cells // LANES
    subs = recv.shape[0]
    pack = LANES // snaps
    part = snaps // n_grp
    cut = LANES // QUAD
    rows_t = snaps // QUAD
    whole, odd = units // QUAD, units % QUAD
    slots = whole + min(odd, 1)
    spare = blocks - whole
    fixed = floor if spare else slots
    middle = snaps // 2
    bottom, top = pl.ds(0, middle), pl.ds(middle, middle)
    short_rows = pl.ds(0, odd * rows_t)
    quarter = iota((1, 1, LANES), 2) // cut
    table = slot_table(slots, n_sec, subs)
    core, xbit, ybit = n_role, 1, 2 * n_role
    if spare:
        pools, stage, wall, home_sem, keep_sem, ls_sem, lr_sem, lt_sem, ws_sem, wr_sem = (
            extra[:spare], *extra[spare:])


    def at_plane(g):
        return {"tile": g // n_role, "role": g % n_role}

    barrier = pltpu.get_barrier_semaphore()
    for o in range(1, n_sec):
        pl.semaphore_signal(barrier, inc=1, device_id={"sec": lax.rem(me + o, n_sec)}, device_id_type=MESH)
    for o in range(1, n_grp):
        pl.semaphore_signal(barrier, inc=1, device_id=at_plane(lax.rem(grp + o, n_grp)), device_id_type=MESH)
    pl.semaphore_wait(barrier, n_sec + n_grp - 2)

    def piece(j):
        return p_ref.at[:, :, pl.ds(j * LANES, LANES)]

    def content(j):
        if j < fixed:
            return piece(j)
        return stage.at[j - fixed] if j < whole else stage.at[j - fixed, short_rows]

    def target(j):
        return recv.at[table[j][1], me] if j < whole else recv.at[table[j][1], me, short_rows]

    def owner(j):
        z = table[j][0]
        return z + side * (n_sec - 1 - 2 * z)

    def outgoing(j):
        sub = table[j][1]
        return pltpu.make_async_remote_copy(
            src_ref=content(j), dst_ref=target(j),
            send_sem=send_sem.at[j], recv_sem=recv_sem.at[sub, me],
            device_id={"sec": owner(j)}, device_id_type=MESH)

    def own(j):
        sub = table[j][1]
        return pltpu.make_async_copy(content(j), target(j), own_sem.at[sub])

    def is_far(j):
        return owner(j) // (n_sec // 2) != me // (n_sec // 2)

    def launch(js):
        for j in js:
            @pl.when(is_far(j))
            def _():
                outgoing(j).start()
        for j in js:
            @pl.when(jnp.logical_and(jnp.logical_not(is_far(j)), owner(j) != me))
            def _():
                outgoing(j).start()

            @pl.when(owner(j) == me)
            def _():
                own(j).start()

    launch(range(fixed))

    order = stage_blocks(units, blocks)
    if spare:
        least, most = QUAD * fixed, QUAD * blocks
        count = [jnp.maximum((live_ref[g] + (cut - 1)) // cut, least) for g in range(n_grp)]
        shape = (-(-(most - units) // SUB) * SUB, LANES)
        unit_of, grp_of = units + iota(shape, 0), iota(shape, 1)
        place_of, given = jnp.zeros(shape, jnp.int32), jnp.zeros(shape, jnp.int32)
        supply = jnp.int32(0)
        low_of, base_of = jnp.zeros(shape, jnp.int32), jnp.zeros(shape, jnp.int32)
        for b in order:
            low, high = max(units, QUAD * b), QUAD * (b + 1)
            here = unit_of // QUAD == b
            low_of = jnp.where(here, low, low_of)
            base_of = jnp.where(here, supply, base_of)
            for g in range(n_grp):
                supply += jnp.maximum(jnp.minimum(count[g], high) - low, 0)
        for g in range(n_grp):
            more = jnp.where(count[g] > unit_of, 1, 0)
            given += jnp.where(grp_of == g, more, 0)
            place_of += jnp.maximum(jnp.minimum(unit_of, count[g]) - low_of, 0) + jnp.where(grp_of > g, more, 0)
        gap = sum(jnp.maximum(units - count[g], 0) for g in range(n_grp)) - supply
        key_of = jnp.where(given == 1, base_of + place_of, -most * n_grp)

    def plan(u):
        home_count, want = jnp.int32(0), jnp.int32(0)
        for g in range(n_grp):
            home_count += jnp.where(grp == g, count[g], 0)
            want += jnp.maximum(u - count[g], 0) + jnp.where(jnp.logical_and(g < grp, count[g] <= u), 1, 0)
        want -= gap
        code = jnp.sum(jnp.where(key_of == want, n_grp * unit_of + grp_of, 0))
        home = u < home_count
        used = jnp.where(home, 1, jnp.where(jnp.logical_and(want >= 0, want < supply), 1, 0))
        return jnp.where(home, n_grp * u + grp, code), used, jnp.where(home, 0, used)

    def turn(x, amount, axis):
        x = jnp.where(amount % 2 == 1, pltpu.roll(x, cut, axis), x)
        return jnp.where(amount // 2 == 1, pltpu.roll(x, 2 * cut, axis), x)

    if spare:
        gx, gy, gc = flip(grp, xbit), flip(grp, ybit), flip(grp, core)
        gxy = flip(gx, ybit)
        offset = slots - fixed

        def place(k, g):
            return pools[k].at[g + (offset if k == 0 else 0)]

        hops = [(grp, gx, bottom), (grp, gy, top), (grp, gx, top), (grp, gy, bottom), (grp, gc, None),
                (gx, gy, bottom), (gy, gx, top), (gx, gc, None), (gy, gc, None), (gxy, gc, None)]

        def hop(k, n):
            origin, to, at = hops[n]
            src = piece(order[k]) if n < 5 else place(k, origin)
            dst = place(k, origin)
            if at is not None:
                src, dst = src.at[at], dst.at[at]
            arrival = lr_sem.at[k, origin] if at is not top else lt_sem.at[k, origin]
            return pltpu.make_async_remote_copy(
                src_ref=src, dst_ref=dst, send_sem=ls_sem.at[k, n], recv_sem=arrival,
                device_id=at_plane(to), device_id_type=MESH)

        def came(k, origin, at=None):
            dst = place(k, origin)
            if at is not None:
                dst = dst.at[at]
            arrival = lr_sem.at[k, origin] if at is not top else lt_sem.at[k, origin]
            pltpu.make_async_remote_copy(
                src_ref=dst, dst_ref=dst, send_sem=ls_sem.at[k, 0], recv_sem=arrival,
                device_id=at_plane(gx), device_id_type=MESH).wait_recv()

        def keep(k):
            return pltpu.make_async_copy(piece(order[k]), place(k, grp), keep_sem.at[k])

        def hold(j):
            return pltpu.make_async_copy(piece(j), pools[0].at[j - fixed], home_sem.at[j - fixed])

        def weight_to(o):
            return pltpu.make_async_remote_copy(
                src_ref=w_ref, dst_ref=wall.at[grp],
                send_sem=ws_sem.at[o], recv_sem=wr_sem.at[grp],
                device_id=at_plane(lax.rem(grp + o, n_grp)), device_id_type=MESH)

        def weight_from(o):
            other = lax.rem(grp + o, n_grp)
            return pltpu.make_async_remote_copy(
                src_ref=w_ref, dst_ref=wall.at[other],
                send_sem=ws_sem.at[o], recv_sem=wr_sem.at[other],
                device_id=at_plane(other), device_id_type=MESH)

        for n in range(5):
            hop(0, n).start()
        for j in range(fixed, slots):
            hold(j).start()
        for k in range(spare):
            keep(k).start()
        for o in range(1, n_grp):
            weight_to(o).start()
        wall[grp] = w_ref[...]

    acc[...] = jnp.zeros(acc.shape, F32)

    @pl.loop(0, snaps * SUB // 16)
    def _(i):
        at = pl.multiple_of(i * 16, 16)
        ttab[pl.ds(at, 16), :] = left_terms(time_terms(snaps, at, 16))

    @pl.loop(0, angles // LANES)
    def _(i):
        at = pl.multiple_of(i * LANES, LANES)
        hi, lo = halves(angle_terms(mode_ref[...], angles, at, LANES))
        for n, x in enumerate((hi, hi, lo)):
            atab[:, pl.ds(n * angles + at, LANES)] = x

    late = partner(n_sec - 1, me, n_sec)
    late_at = pl.multiple_of(late * q_loc, SUB)
    ltab[...] = left_terms(angle_terms(mode_ref[...], angles, late_at, q_loc))
    total = float(cells * n_grp)

    if spare:
        def source(u, depth):
            code, _, foreign = plan(u)
            unit, g = code // n_grp, code % n_grp
            block = unit // QUAD
            first = jnp.where(jnp.logical_and(foreign == 1, block == order[0]), g + offset, u // QUAD - fixed)

            def read(t, to):
                x = pools[0][first, pl.ds(t, 1)]
                for k in range(1, depth + 1):
                    x = jnp.where(jnp.logical_and(foreign == 1, block == order[k]), pools[k][g, pl.ds(t, 1)], x)
                return turn(x, (to + QUAD - unit % QUAD) % QUAD, 2)
            return read

        def fill(j, depth):
            if j < whole:
                reads = [source(QUAD * j + i, depth) for i in range(QUAD)]

                @pl.loop(0, snaps)
                def _(t):
                    x = reads[0](t, 0)
                    for i in range(1, QUAD):
                        x = jnp.where(quarter == i, reads[i](t, i), x)
                    stage[j - fixed, pl.ds(t, 1)] = x
                return
            for i in range(odd):
                read = source(QUAD * j + i, depth)

                @pl.loop(0, rows_t)
                def _(r):
                    x = read(r, 0)
                    for b in range(1, QUAD):
                        x = jnp.where(quarter == b, read(b * rows_t + r, b), x)
                    stage[j - fixed, pl.ds(i * rows_t + r, 1)] = x

        def advance(k):
            came(k, gx, bottom)
            hop(k, 5).start()
            came(k, gy, top)
            hop(k, 6).start()
            if k + 1 < spare:
                for n in range(5):
                    hop(k + 1, n).start()
            came(k, gx, top)
            hop(k, 7).start()
            came(k, gy, bottom)
            hop(k, 8).start()
            came(k, gxy, bottom)
            came(k, gxy, top)
            hop(k, 9).start()
            for g in (gc, flip(gx, core), flip(gy, core), flip(gxy, core)):
                came(k, g)
            keep(k).wait()
            if k == 0:
                for j in range(fixed, slots):
                    hold(j).wait()
            for j in range(fixed, slots):
                if min(j - fixed, spare - 1) == k:
                    fill(j, k)
                    launch([j])

        for k in range(min(spare, 2)):
            advance(k)
        for o in range(1, n_grp):
            weight_from(o).wait_recv()

    rank = me + side * (n_sec - 1 - 2 * me)

    def holding(sub):
        slot, have = jnp.int32(0), jnp.int32(0)
        for j, (z, at) in enumerate(table):
            hit = jnp.logical_and(rank == z, sub == at)
            slot += jnp.where(hit, j, 0)
            have += jnp.where(hit, 1, 0)
        return slot, have

    def weight_row(slot):
        lane = iota((1, LANES), 1)
        row = iota((blocks, LANES), 0)
        if not spare:
            w = jnp.sum(jnp.where(row == slot, w_ref[...], 0.0), axis=0, keepdims=True)
            return jnp.where(slot * LANES + lane < live_ref[grp], w / total, 0.0)

        def unit_row(i):
            code, used, _ = plan(QUAD * slot + i)
            unit, g = code // n_grp, code % n_grp
            live = jnp.int32(0)
            w = jnp.zeros((blocks, LANES), F32)
            for h in range(n_grp):
                live += jnp.where(g == h, live_ref[h], 0)
                w += jnp.where(row == jnp.where(g == h, unit // QUAD, -1), wall[h], 0.0)
            w = jnp.sum(turn(w, (i + QUAD - unit % QUAD) % QUAD, 1), axis=0, keepdims=True)
            if odd and i >= odd:
                used = jnp.where(slot < whole, used, 0)
            return jnp.where(unit * cut + lane % cut < jnp.where(used == 1, live, 0), w / total, 0.0)

        w = unit_row(0)
        for i in range(1, QUAD):
            w = jnp.where(lane // cut == i, unit_row(i), w)
        return w

    wide = 2

    def to_spectra(j, src):
        @pl.loop(0, q_loc // (wide * SUB), unroll=2)
        def _(i):
            g = pl.multiple_of(i * (wide * SUB), wide * SUB)
            x = jnp.concatenate(
                [recv[j, src, :, pl.ds(g + u * SUB, SUB), :].reshape(snaps * SUB, LANES) for u in range(wide)],
                axis=1)
            y = dot(ttab[...], right_terms(x))
            for u in range(wide):
                at = pl.multiple_of(src * q_loc + g + u * SUB, SUB)
                spec[:, pl.ds(at, SUB), :] = y[:, u * LANES:(u + 1) * LANES].reshape(snaps, SUB, LANES)

    stage_rows = acc.shape[1] // STAGES

    def pair(t):
        at = pl.ds(pl.multiple_of(t * stage_rows, SUB), stage_rows)
        return pltpu.make_async_remote_copy(
            src_ref=acc.at[pl.ds((1 - side) * near, near), at, :], dst_ref=pbuf.at[:, at, :],
            send_sem=pa_sem.at[t], recv_sem=pr_sem.at[t],
            device_id={"tile": tile + 1 - 2 * side}, device_id_type=MESH)

    def share(o, t, arriving=False):
        other = lax.rem(mine + o, near)
        at = pl.ds(pl.multiple_of(t * stage_rows, SUB), stage_rows)
        slot = other if arriving else mine
        return pltpu.make_async_remote_copy(
            src_ref=pacc.at[other, at, :], dst_ref=reda.at[slot, at, :],
            send_sem=sa_sem.at[t, other], recv_sem=ra_sem.at[t, slot],
            device_id={"tile": other // n_role * 2 + side, "role": other % n_role}, device_id_type=MESH)

    def forward(t):
        pair(t).wait_recv()
        at = pl.ds(pl.multiple_of(t * stage_rows, SUB), stage_rows)
        pacc[:, at, :] = acc[pl.ds(side * near, near), at, :] + pbuf[:, at, :]
        for o in range(1, near):
            share(o, t).start()

    def unpack(j, src):
        @pl.loop(0, rows_t)
        def _(r):
            packed = [recv[j, src, pl.ds(i * rows_t + r, 1)] for i in range(odd)]
            for b in range(QUAD):
                x = pltpu.roll(packed[0], (QUAD - b) % QUAD * cut, 2) if b else packed[0]
                for i in range(1, odd):
                    move = (i + QUAD - b) % QUAD * cut
                    x = jnp.where(quarter == i, pltpu.roll(packed[i], move, 2) if move else packed[i], x)
                recv[j, src, pl.ds(b * rows_t + r, 1)] = x

    def landed(j, src, short):
        def wait(dst):
            pltpu.make_async_remote_copy(
                src_ref=dst, dst_ref=dst, send_sem=send_sem.at[0], recv_sem=recv_sem.at[j, src],
                device_id={"sec": src}, device_id_type=MESH).wait_recv()

        if not odd:
            wait(recv.at[j, src])
            return

        @pl.when(short)
        def _():
            wait(recv.at[j, src, short_rows])
            unpack(j, src)

        @pl.when(jnp.logical_not(short))
        def _():
            wait(recv.at[j, src])

    def landed_own(j, short):
        def wait(dst):
            pltpu.make_async_copy(dst, dst, own_sem.at[j]).wait()

        if not odd:
            wait(recv.at[j, me])
            return

        @pl.when(short)
        def _():
            wait(recv.at[j, me, short_rows])
            unpack(j, me)

        @pl.when(jnp.logical_not(short))
        def _():
            wait(recv.at[j, me])

    def arrive(i, j, short):
        src = partner(i, me, n_sec)
        landed(j, src, short)
        to_spectra(j, src)

    def to_modal(f, y):
        zbuf[pl.ds(f, modes, stride=snaps), :] = y[:modes, :LANES] + y[modes:, LANES:]
        zbuf[pl.ds(half + f, modes, stride=snaps), :] = y[:modes, LANES:] - y[modes:, :LANES]

    def products(f):
        x = jnp.concatenate([spec[f], spec[half + f]], axis=1)
        return dot(atab[...], right_terms(x))

    def process(j, slot):
        short = slot >= whole
        landed_own(j, short)
        to_spectra(j, me)

        @pl.loop(1, n_sec - 1)
        def _(i):
            arrive(i, j, short)

        spec[:, pl.ds(late_at, q_loc), :] = jnp.zeros((snaps, q_loc, LANES), F32)

        @pl.loop(0, half)
        def _(f):
            ypart[f] = products(f)

        weight = weight_row(slot)
        arrive(n_sec - 1, j, short)

        @pl.loop(0, half, unroll=UNROLL)
        def _(f):
            x = jnp.concatenate([spec[f, pl.ds(late_at, q_loc), :], spec[half + f, pl.ds(late_at, q_loc), :]], axis=1)
            to_modal(f, ypart[f] + dot(ltab[...], right_terms(x)))

        block = iota((snaps, LANES), 1) // snaps
        steps = SUB // part

        def gram(h):
            rows = []
            for u in range(steps):
                at = pl.multiple_of((h * steps + u) * LANES, LANES)
                z = zbuf[pl.ds(at, LANES), :]
                zh, zl = halves(z)
                g4 = dot(left_terms(z * weight), jnp.concatenate([zh, zl, zh], axis=1), (((1,), (1,)), ((), ())))
                r = g4[:snaps]
                for b in range(1, pack):
                    r = jnp.where(block == b, g4[b * snaps:(b + 1) * snaps], r)
                rows.append(r)
            at = pl.multiple_of(h * SUB, SUB)
            for g in range(n_grp):
                new = jnp.concatenate([r[g * part:(g + 1) * part] for r in rows], axis=0)
                to = g // n_role % 2 * near + g // n_role // 2 * n_role + g % n_role
                acc[to, pl.ds(at, SUB), :] += new

        size = modes // pack // steps // STAGES

        @pl.loop(0, STAGES)
        def _(t):
            pl.loop(0, size, unroll=UNROLL)(lambda h: gram(t * size + h))

            @pl.when(j == subs - 1)
            def _():
                pair(t).start()

            @pl.when(jnp.logical_and(j == subs - 1, t > 0))
            def _():
                forward(t - 1)

    @pl.loop(0, subs)
    def _(j):
        slot, have = holding(j)
        pl.when(have == 1)(functools.partial(process, j, slot))
        if spare > 2:
            pl.when(j == 0)(functools.partial(advance, 2))

    def last(s, slot):
        return pltpu.make_async_remote_copy(
            src_ref=sb.at[s], dst_ref=redb.at[slot],
            send_sem=sb_sem.at[s], recv_sem=rb_sem.at[slot],
            device_id={"sec": s}, device_id_type=MESH)

    forward(STAGES - 1)
    rows = sb.shape[1]
    for t in range(STAGES):
        for o in range(1, near):
            share(o, t, True).wait_recv()
        for s in range(t * n_sec // STAGES, (t + 1) * n_sec // STAGES):
            value = pacc[mine, s * rows:(s + 1) * rows, :]
            for o in range(1, near):
                value += reda[lax.rem(mine + o, near), s * rows:(s + 1) * rows, :]
            sb[s] = value

            @pl.when(me != s)
            def _():
                last(s, me).start()

    value = sb[me]
    for o in range(1, n_sec):
        s = lax.rem(me + o, n_sec)
        last(s, s).wait_recv()
        value += redb[s]
    out_ref[...] = value

    for j in range(slots):
        @pl.when(owner(j) != me)
        def _():
            outgoing(j).wait_send()
    if spare:
        for k in range(spare):
            for n in range(len(hops)):
                hop(k, n).wait_send()
        for o in range(1, n_grp):
            weight_to(o).wait_send()
    for t in range(STAGES):
        pair(t).wait_send()
        for o in range(1, near):
            share(o, t).wait_send()
    for o in range(1, n_sec):
        last(lax.rem(me + o, n_sec), me).wait_send()


def choose(blocks, floor, live_ref, out_ref):
    cut, top, least = LANES // QUAD, QUAD * blocks, QUAD * floor
    n_grp = live_ref.shape[0]
    count = [jnp.maximum((live_ref[g] + (cut - 1)) // cut, least) for g in range(n_grp)]
    above = {u: sum(jnp.where(c > u, 1, 0) for c in count) for u in range(least, top)}

    def fits(units):
        whole = units // QUAD
        spare = blocks - whole
        stages = [sum(above[u] for u in range(max(units, QUAD * b), QUAD * (b + 1))) for b in stage_blocks(units, blocks)]
        good = sum(stages) <= sum(n_grp - above[u] for u in range(least, units))
        for k in range(1, spare):
            space = sum(n_grp - above[u] for u in range(least + QUAD * k, units))
            good = jnp.logical_and(good, sum(stages[k:]) <= space)
        return good

    pick = jnp.int32(0)
    for number, less in enumerate(VARIANTS):
        if number:
            pick = jnp.where(fits(top - less), number, pick)
    out_ref[0] = pick


def on_device(pressure, cell_weight, live_cells, mode_order):
    n_sec, n_tile, n_role = (lax.axis_size(a) for a in ("sec", "tile", "role"))
    n_grp = n_tile * n_role
    snaps, q_loc, cells = pressure.shape
    modes = mode_order.shape[0]
    angles = q_loc * n_sec
    blocks = cells // LANES
    subs = blocks // n_sec
    pack = LANES // snaps
    part = snaps // n_grp
    rows = modes // pack * part
    own_rows = rows // n_sec
    vmem = pl.BlockSpec(memory_space=pltpu.VMEM)
    dma = pltpu.SemaphoreType.DMA
    adaptive = subs == 2 and n_grp == blocks and n_role == 2 and n_sec == 4 and q_loc % 16 == 0
    floor = -(-(cells // 3) // LANES)

    def scratch(units):
        whole = units // QUAD
        slots = whole + min(units % QUAD, 1)
        shapes = [
            pltpu.VMEM((subs, n_sec, snaps, q_loc, LANES), F32),
            pltpu.VMEM((snaps, angles, LANES), F32),
            pltpu.VMEM((modes * snaps, LANES), F32),
            pltpu.VMEM((n_grp, rows, LANES), F32),
            pltpu.VMEM((n_grp // 2, rows, LANES), F32),
            pltpu.VMEM((n_grp // 2, rows, LANES), F32),
            pltpu.VMEM((n_grp // 2, rows, LANES), F32),
            pltpu.VMEM((n_sec, own_rows, LANES), F32),
            pltpu.VMEM((n_sec, own_rows, LANES), F32),
            pltpu.VMEM((snaps * SUB, 3 * snaps * SUB), BF16),
            pltpu.VMEM((2 * modes, 3 * angles), BF16),
            pltpu.VMEM((2 * modes, 3 * q_loc), BF16),
            pltpu.VMEM((snaps // 2, 2 * modes, 2 * LANES), F32),
            dma((slots,) if adaptive else (subs, n_sec)), dma((subs, n_sec)), dma((subs,)),
            dma((STAGES,)), dma((STAGES,)), dma((STAGES, n_grp // 2)), dma((STAGES, n_grp // 2)), dma((n_sec,)), dma((n_sec,)),
        ]
        spare = blocks - whole
        if adaptive and spare:
            block = (snaps, q_loc, LANES)
            extra = slots - floor
            shapes += [pltpu.VMEM((n_grp + (extra if k == 0 else 0), *block), F32) for k in range(spare)]
            shapes += [
                pltpu.VMEM((extra, *block), F32),
                pltpu.VMEM((n_grp, blocks, LANES), F32),
                dma((extra,)), dma((spare,)), dma((spare, 10)), dma((spare, n_grp)), dma((spare, n_grp)), dma((n_grp,)), dma((n_grp,)),
            ]
        return shapes

    def call(units, number=0):
        body = functools.partial(ragged, units, floor) if adaptive else kernel
        return pl.pallas_call(
            functools.partial(body, n_sec, n_tile, n_role),
            out_shape=jax.ShapeDtypeStruct((own_rows, LANES), F32),
            in_specs=[pl.BlockSpec(memory_space=pl.ANY), vmem, pl.BlockSpec(memory_space=pltpu.SMEM), vmem],
            out_specs=vmem,
            scratch_shapes=scratch(units),
            compiler_params=pltpu.CompilerParams(
                collective_id=number, has_side_effects=True, vmem_limit_bytes=62 * 2**20),
            name="spod",
        )

    args = (pressure, cell_weight.reshape(blocks, LANES), live_cells, mode_order.reshape(1, modes))
    if adaptive:
        top = QUAD * blocks
        pick = pl.pallas_call(
            functools.partial(choose, blocks, floor),
            out_shape=jax.ShapeDtypeStruct((1,), jnp.int32),
            in_specs=[pl.BlockSpec(memory_space=pltpu.SMEM)],
            out_specs=pl.BlockSpec(memory_space=pltpu.SMEM),
            name="choose",
        )(live_cells)[0]
        packed = lax.switch(pick, [call(top - less, number) for number, less in enumerate(VARIANTS)], *args)
    else:
        packed = call(QUAD * blocks)(*args)
    out = packed.reshape(modes // pack // n_sec, part, pack, snaps)
    return out.transpose(0, 2, 1, 3).reshape(modes // n_sec, part, snaps)


def solution(mesh):
    in_specs = (P(None, "sec", ("tile", "role")), P(("tile", "role")), P(), P())
    out_specs = P("sec", ("tile", "role"), None)
    return jax.shard_map(
        on_device, mesh=mesh, in_specs=in_specs, out_specs=out_specs, check_vma=False
    )
```
